32 devices in a mesh: groups: 2 (over y), dp: 16 (over z, x, core).
Axes of the slice: x: 2, y: 2, z: 4, core: 2. Of those that a mesh axis runs over, the one named last changes fastest.
Arguments:
- query_acts: bfloat16 [4096, 8192], P(('groups', 'dp')), parts along dimension 0, may hold values from -6 to 6
- cotangent: bfloat16 [4096, 8192], P(('groups', 'dp')), parts along dimension 0, may hold values from -6 to 6
- conv_weight: float32 [4, 4, 8192], replicated, may hold values from -3 to 3
- conv_bias: float32 [4, 8192], replicated, may hold values from -3 to 3
- owner_map: int32 [4], replicated, may hold values from 0 to 15, as said below
- basis_store: float32 [16, 25, 8192], P('dp'), may hold values from -2.5 to 2.5
- lambda_store: float32 [16, 5, 8192], P('dp'), may hold values from 0.1 to 10
- train_grads: bfloat16 [256, 4, 5, 8192], P(('groups', 'dp')), parts along dimension 0, may hold values from -6 to 6
- batch_index: int32 [512], P(('groups', 'dp')), parts along dimension 0, may hold values from 0 to 127, as said below
Outputs:
- adjoint_in: bfloat16 [4096, 8192], P(('groups', 'dp')), parts along dimension 0
- scores: float32 [512], P(('groups', 'dp')), parts along dimension 0
The draws below stay inside these ranges and needn't reach their ends.
There are 2 independent parts, one for each index of `groups`. The reference program is written for one: setup_inputs(seed, part) draws one part's arguments, and reference() takes and returns one part's arrays. A program takes and returns all parts, laid end to end along the dimension named above; an argument that names none is the same for every part. Nothing has to cross between parts.
Inputs may be any that keep to these rules, and one draw needn't show every extreme that they name: `owner_map`: the 4 entries are distinct. `batch_index`: entry n names a row from (n // 16) * 8 to (n // 16) * 8 + 7.
All inputs are finite; a program needn't handle non-finite values.
Results may differ from the reference program's by a relative error of at most 0.015.
Values may be sent and summed in bfloat16 or wider, within the bound.
A program may use at most 128 MiB of HBM per device.

```python
import math
import jax
import jax.numpy as jnp
from jax import lax

C = 8192
LAYERS = 4
E_DEV = 8
B_DEV = 16
TOKENS = 2048
TRAIN = 128
BATCH = 256
SLOTS = 16


def draw_owner_map(key, part):
    middle = jax.random.permutation(jax.random.fold_in(key, 1), SLOTS - 2)[:LAYERS - 2].astype(jnp.int32) + 1
    owners = jnp.concatenate([jnp.array([0, SLOTS - 1], dtype=jnp.int32), middle])
    order = jax.random.permutation(jax.random.fold_in(key, 2), LAYERS)
    return owners[order].astype(jnp.int32)


def draw_batch_index(key, part):
    base = jnp.arange(BATCH, dtype=jnp.int32) // B_DEV * E_DEV
    offsets = jax.random.randint(key, (BATCH,), 0, E_DEV, dtype=jnp.int32)
    offsets = offsets.at[0].set(0).at[BATCH - 1].set(E_DEV - 1)
    return (base + offsets).astype(jnp.int32)


def level_of(key, shape, pieces, least, largest):
    factor_of, own = 1.0, jax.random.fold_in(key, 6)
    for axis_at, blocks in pieces:
        steps = jnp.exp(jax.random.uniform(jax.random.fold_in(own, axis_at), (blocks,), jnp.float32, least / len(pieces), largest / len(pieces)))
        factor_of = factor_of * jnp.repeat(steps, shape[axis_at] // blocks).reshape([-1 if axis == axis_at else 1 for axis in range(len(shape))])
    return factor_of


def bell_draw(key, extent, scale, bound, split=(), kind=jnp.bfloat16):
    drawn = jax.random.normal(key, extent, jnp.float32) * scale
    if len(split) > 0:
        drawn = level_of(key, extent, split, -0.22, 0.18) * drawn
    return jnp.clip(drawn, min=-bound, max=bound).astype(kind)


def setup_inputs(seed: int = 0, part: int = 0) -> dict:
    splits = jax.random.split(jax.random.key(seed), 10)
    part_keys = jax.random.split(jax.random.fold_in(splits[9], part), 10)
    return {
        "query_acts": bell_draw(part_keys[0], (TOKENS, C), 1.0, 6.0, ((0, 16),)),
        "cotangent": bell_draw(part_keys[1], (TOKENS, C), 1.0, 6.0, ((0, 16),)),
        "conv_weight": bell_draw(splits[2], (LAYERS, 4, C), 4 ** -0.5, 3.0, (), jnp.float32),
        "conv_bias": bell_draw(splits[3], (LAYERS, C), 0.5, 3.0, (), jnp.float32),
        "owner_map": draw_owner_map(jax.random.fold_in(splits[9], 71), part),
        "basis_store": bell_draw(splits[5], (SLOTS, 25, C), 5 ** -0.5, 2.5, ((0, 16),), jnp.float32),
        "lambda_store": jnp.clip(jnp.exp(math.log(10.0) - 4.6051702 * jax.random.uniform(splits[6], (SLOTS, 5, C), jnp.float32) ** level_of(splits[6], (SLOTS, 5, C), ((0, 16),), -0.2, 0.2)), 0.1, 10.0),
        "train_grads": bell_draw(part_keys[7], (TRAIN, LAYERS, 5, C), 1.0, 6.0, ((0, 16),)),
        "batch_index": draw_batch_index(jax.random.fold_in(jax.random.fold_in(splits[9], part), 71), part),
    }


def convolve(padded, weights, bias, count):
    result = jnp.broadcast_to(bias[None, :], (count, bias.shape[0]))
    for offset in range(4):
        result = result + weights[offset][None, :] * padded[3 - offset:3 - offset + count].astype(jnp.float32)
    return result

def silu_slope(values):
    sig = jax.nn.sigmoid(values)
    return sig * (1.0 + values * (1.0 - sig))

def precondition(gradient, eigen_basis, eigen_vals):
    damping = 0.1 * jnp.mean(eigen_vals)
    rotated = lax.optimization_barrier(jnp.sum(eigen_basis * gradient[:, None, :], axis=0))
    scaled = rotated / (eigen_vals + damping)
    return lax.optimization_barrier(jnp.sum(eigen_basis * scaled[None, :, :], axis=1))

def window(acts, cot, weights, bias):
    count = acts.shape[0]
    width = acts.shape[1]
    stream = acts
    saved = []
    for layer_id in range(LAYERS):
        padded = jnp.concatenate([jnp.zeros((3, width), jnp.bfloat16), stream], axis=0)
        saved.append(padded)
        conv_out = convolve(padded, weights[layer_id], bias[layer_id], count)
        stream = (stream.astype(jnp.float32) + jax.nn.silu(conv_out)).astype(jnp.bfloat16)
    adjoint = cot
    partials = [None] * LAYERS
    for layer_id in reversed(range(LAYERS)):
        padded = saved[layer_id]
        conv_out = convolve(padded, weights[layer_id], bias[layer_id], count)
        conv_grad = (adjoint.astype(jnp.float32) * silu_slope(conv_out)).astype(jnp.bfloat16)
        grad_f = conv_grad.astype(jnp.float32)
        terms = [lax.optimization_barrier(jnp.sum(padded[3 - offset:3 - offset + count].astype(jnp.float32) * grad_f, axis=0)) for offset in range(4)]
        terms.append(lax.optimization_barrier(jnp.sum(grad_f, axis=0)))
        partials[layer_id] = jnp.stack(terms)
        extended = jnp.concatenate([conv_grad, jnp.zeros((3, width), jnp.bfloat16)], axis=0)
        conv_back = jnp.zeros((count, width), jnp.float32)
        for offset in range(4):
            conv_back = conv_back + weights[layer_id, offset][None, :] * extended[offset:offset + count].astype(jnp.float32)
        adjoint = (adjoint.astype(jnp.float32) + conv_back).astype(jnp.bfloat16)
    return (adjoint, jnp.stack(partials))

def reference(query_acts, cotangent, conv_weight, conv_bias, owner_map, basis_store, lambda_store, train_grads, batch_index):
    width = 128
    blocks = C // width
    acts_blocks = query_acts.reshape(TOKENS, blocks, width).transpose(1, 0, 2)
    cot_blocks = cotangent.reshape(TOKENS, blocks, width).transpose(1, 0, 2)
    weight_blocks = conv_weight.reshape(LAYERS, 4, blocks, width).transpose(2, 0, 1, 3)
    bias_blocks = conv_bias.reshape(LAYERS, blocks, width).transpose(1, 0, 2)
    adjoint_blocks, grad_blocks = lax.map(lambda packed: window(packed[0], packed[1], packed[2], packed[3]), (acts_blocks, cot_blocks, weight_blocks, bias_blocks))
    adjoint_in = adjoint_blocks.transpose(1, 0, 2).reshape(TOKENS, C)
    gradients = grad_blocks.transpose(1, 2, 0, 3).reshape(LAYERS, 5, C) * (1.0 / math.sqrt(TOKENS))
    corrected = []
    for layer_id in range(LAYERS):
        owner = owner_map[layer_id]
        eigen_basis = basis_store[owner].reshape(5, 5, C)
        eigen_vals = lambda_store[owner]
        corrected.append(precondition(gradients[layer_id], eigen_basis, eigen_vals))
    flattened = jnp.stack(corrected).reshape(-1)
    high_part = flattened.astype(jnp.bfloat16)
    low_part = (flattened - high_part.astype(jnp.float32)).astype(jnp.bfloat16)
    both_parts = jnp.stack([high_part, low_part], axis=1).astype(jnp.float32)
    rows_view = train_grads.reshape(SLOTS, E_DEV, LAYERS * 5 * C)
    all_scores = lax.map(lambda block_rows: lax.optimization_barrier(jnp.sum(jnp.dot(block_rows.astype(jnp.float32), both_parts, precision=lax.Precision.HIGHEST), axis=1)), rows_view).reshape(TRAIN)
    all_scores = all_scores * (1.0 / math.sqrt(5 * LAYERS * C))
    scores = all_scores[batch_index]
    return (adjoint_in, scores)
```

```python
import functools
import math

import jax
import jax.numpy as jnp
import numpy as np
from jax import lax
from jax.experimental import pallas as pl
from jax.experimental.pallas import tpu as pltpu
from jax.sharding import PartitionSpec as P

LANES = 128
SUB = 8
TAPS = 4
HALO_ROWS = 16
PAIRS = [(j, k) for j in range(5) for k in range(j, 5)]


def layout_plan(rows, layers):
    reach = (TAPS - 1) * layers
    extended = rows + 2 * reach
    fold = -(-extended // SUB)
    padded = -(-(fold * SUB) // 16) * 16
    return reach, fold, padded


def permutations(rows, layers):
    reach, fold, padded = layout_plan(rows, layers)
    columns = rows + 2 * HALO_ROWS
    into = np.zeros((padded, columns), np.float32)
    back = np.zeros((rows, padded), np.float32)
    for j in range(fold):
        for s in range(SUB):
            token = fold * s + j - reach
            row = SUB * j + s
            if 0 <= token < rows:
                into[row, token] = 1.0
                back[token, row] = 1.0
            elif -reach <= token < 0:
                into[row, rows + HALO_ROWS + token] = 1.0
            elif rows <= token < rows + reach:
                into[row, HALO_ROWS + token] = 1.0
    return jnp.asarray(into, jnp.bfloat16), jnp.asarray(back, jnp.bfloat16)


def rounded(value):
    return value.astype(jnp.bfloat16).astype(jnp.float32)


def window_chunk(lanes, rows, layers, is_first, w_ref, b_ref, x_all, c_all, slope_all, g_ref):
    reach, fold, padded = layout_plan(rows, layers)
    sub = lax.broadcasted_iota(jnp.int32, (SUB, LANES), 0)
    edges = {}

    def own(j, low, high):
        tokens = [fold * s + j - reach for s in range(SUB)]
        inside = tuple(low <= t < high for t in tokens)
        if all(inside):
            return None
        if inside not in edges:
            lead = next(i for i, ok in enumerate(inside) if ok)
            tail = max(i for i, ok in enumerate(inside) if ok)
            edges[inside] = (sub >= lead) & (sub <= tail)
        return edges[inside]

    zero = jnp.zeros((SUB, LANES), jnp.float32)

    def keep(value, mask):
        return value if mask is None else jnp.where(mask, value, zero)

    def row(ref, *at):
        return jnp.broadcast_to(ref[at[:-1] + (pl.ds(at[-1], 1), lanes)], (SUB, LANES))

    live = {}

    def begun(j):
        mask = own(j, 0, 1 << 30)
        if mask is None:
            return None
        key = id(mask)
        if key not in live:
            live[key] = mask | jnp.logical_not(is_first)
        return live[key]

    last = TAPS - 1
    for layer in range(layers):
        taps = [row(w_ref, layer, k) * 0.5 for k in range(TAPS)]
        bias = row(b_ref, layer) * 0.5
        base = layer * (fold + last) * SUB
        for i in range(last):
            wrapped = x_all[pl.ds(base + (fold + i) * SUB, SUB), lanes]
            x_all[pl.ds(base + i * SUB, SUB), lanes] = pltpu.roll(wrapped, 1, 0)
        x = [x_all[pl.ds(base + i * SUB, SUB), lanes] for i in range(fold + last)]
        following = base + (fold + last + last) * SUB
        for j in range(fold):
            half = bias
            for k in range(TAPS):
                half = half + taps[k] * x[last + j - k]
            bent = jnp.tanh(half)
            up = 1.0 + bent
            slope_all[pl.ds((layer * fold + j) * SUB, SUB), lanes] = up * (1.0 + half * (1.0 - bent))
            if layer < layers - 1:
                fresh = keep(rounded(x[last + j] + half * up), begun(j))
                x_all[pl.ds(following + j * SUB, SUB), lanes] = fresh
    for layer in reversed(range(layers)):
        taps = [row(w_ref, layer, k) * 0.5 for k in range(TAPS)]
        base = layer * (fold + last) * SUB
        doubled = [None] * (fold + last)
        sums = [zero] * (TAPS + 1)

        def at(i):
            return x_all[pl.ds(base + i * SUB, SUB), lanes]

        for j in range(fold):
            adjoint = c_all[pl.ds(j * SUB, SUB), lanes]
            slope = slope_all[pl.ds((layer * fold + j) * SUB, SUB), lanes]
            grad = keep(rounded(adjoint * slope), own(j, 0, 1 << 30))
            doubled[j] = grad
            if j < last:
                doubled[fold + j] = pltpu.roll(grad, SUB - 1, 0)
            inner = keep(grad, own(j, -(1 << 30), rows))
            for k in range(TAPS):
                sums[k] = sums[k] + at(last + j - k) * inner
            sums[TAPS] = sums[TAPS] + inner
        for j in range(fold):
            total = c_all[pl.ds(j * SUB, SUB), lanes]
            back = taps[0] * doubled[j]
            for k in range(1, TAPS):
                back = back + taps[k] * doubled[j + k]
            c_all[pl.ds(j * SUB, SUB), lanes] = rounded(total + back)
        for k in range(TAPS + 1):
            g_ref[pl.ds(layer * 5 + k, 1), lanes] = 0.5 * jnp.sum(sums[k], axis=0, keepdims=True)


def window_kernel(rows, layers, x_ref, c_ref, hx_ref, hc_ref, w_ref, b_ref, into_ref, back_ref,
                  out_ref, g_ref, x_all, c_all, slope_all):
    reach, fold, padded = layout_plan(rows, layers)
    width = x_ref.shape[1]
    is_first = lax.axis_index("dp") == 0
    count = fold * SUB
    acts = jnp.concatenate([x_ref[...], hx_ref[...]], axis=0)
    cots = jnp.concatenate([c_ref[...], hc_ref[...]], axis=0)
    x_all[pl.ds((TAPS - 1) * SUB, count), :] = jnp.dot(
        into_ref[...], acts, preferred_element_type=jnp.float32)[:count]
    c_all[...] = jnp.dot(into_ref[...], cots, preferred_element_type=jnp.float32)

    @pl.loop(0, width // LANES)
    def _(chunk):
        lanes = pl.ds(pl.multiple_of(chunk * LANES, LANES), LANES)
        window_chunk(lanes, rows, layers, is_first, w_ref, b_ref, x_all, c_all, slope_all, g_ref)

    out_ref[...] = jnp.dot(
        back_ref[...], c_all[...].astype(jnp.bfloat16), preferred_element_type=jnp.float32
    ).astype(jnp.bfloat16)


def window(acts, cots, halo_acts, halo_cots, weights, bias):
    rows, channels = acts.shape
    layers = weights.shape[0]
    reach, fold, padded = layout_plan(rows, layers)
    width = 512
    into, back = permutations(rows, layers)
    block = lambda *lead: pl.BlockSpec(lead + (width,), lambda i: (0,) * len(lead) + (i,))
    whole = lambda a: pl.BlockSpec(a.shape, lambda i: (0, 0))
    return pl.pallas_call(
        functools.partial(window_kernel, rows, layers),
        grid=(channels // width,),
        out_shape=(
            jax.ShapeDtypeStruct((rows, channels), jnp.bfloat16),
            jax.ShapeDtypeStruct((layers * 5, channels), jnp.float32),
        ),
        in_specs=[
            block(rows), block(rows), block(2 * HALO_ROWS), block(2 * HALO_ROWS),
            block(layers, TAPS), block(layers), whole(into), whole(back),
        ],
        out_specs=(block(rows), block(layers * 5)),
        scratch_shapes=[
            pltpu.VMEM((layers * (fold + TAPS - 1) * SUB, width), jnp.float32),
            pltpu.VMEM((padded, width), jnp.float32),
            pltpu.VMEM((layers * fold * SUB, width), jnp.float32),
        ],
        compiler_params=pltpu.CompilerParams(vmem_limit_bytes=24 << 20),
        cost_estimate=pl.CostEstimate(flops=200_000_000, bytes_accessed=10_000_000, transcendentals=5_000_000),
    )(acts, cots, halo_acts, halo_cots, weights, bias, into, back)


def shifted(value, axis, steps):
    count = lax.axis_size(axis)
    first, final = (max(0, -steps), min(count, count - steps))
    return lax.ppermute(value, axis, [(s, s + steps) for s in range(first, final)])


def inverse_rows(basis, vals):
    channels = basis.shape[-1]
    blocks = basis.reshape(5, 5, channels)
    scale = 1.0 / (vals + 0.1 * jnp.mean(vals))
    return jnp.stack([jnp.sum(blocks[j] * blocks[k] * scale, axis=0) for j, k in PAIRS])


ROWS8 = 8
HALO = 16


def token_permutation(invert):
    row = lax.broadcasted_iota(jnp.int32, (LANES, LANES), 0)
    col = lax.broadcasted_iota(jnp.int32, (LANES, LANES), 1)
    if invert:
        row, col = col, row
    same = ((row >> 3) == (col & 15)) & ((row & 7) == (col >> 4))
    return jnp.where(same, 1.0, 0.0).astype(jnp.bfloat16)


def forward_layer(layer, layers, rows, step, tile, x_all, s_all, w_all, keep):
    taps = [w_all[layer * TAPS + k, tile, :] * 0.5 for k in range(TAPS)]
    bias = w_all[layers * TAPS + layer, tile, :] * 0.5

    def span(first, n, mask=None):
        x = [x_all[layer, first - 3 + i] for i in range(n + 3)]
        for i in range(n):
            half = ((taps[0] * x[i + 3] + taps[1] * x[i + 2]) + (taps[2] * x[i + 1] + taps[3] * x[i])) + bias
            bent = jnp.tanh(half)
            up = 1.0 + bent
            s_all[layer, first + i] = up * (1.0 + half * (1.0 - bent))
            if layer < layers - 1:
                fresh = x[i + 3] + half * up
                x_all[layer + 1, first + i] = fresh if mask is None else fresh * mask

    early = 3 * (layers - 1 - layer)
    if early:
        span(HALO - early, early, keep)
    total = rows + 3 * layers
    full, rest = total // step, total % step

    @pl.loop(0, full)
    def _(j):
        span(HALO + j * step, step)

    if rest:
        span(HALO + full * step, rest)


def pairwise(values):
    while len(values) > 1:
        values = [values[i] + values[i + 1] if i + 1 < len(values) else values[i]
                  for i in range(0, len(values), 2)]
    return values[0]


def backward_layer(layer, layers, rows, step, tile, x_all, s_all, a_all, w_all, g_all):
    taps = [w_all[layer * TAPS + k, tile, :] * 0.5 for k in range(TAPS)]

    def grads(first, n):
        return [a_all[first + i] * s_all[layer, HALO + first + i] for i in range(n)]

    def back(first, dv, n):
        for i in range(n):
            a_all[first + i] = a_all[first + i] + (
                (taps[0] * dv[i] + taps[1] * dv[i + 1]) + (taps[2] * dv[i + 2] + taps[3] * dv[i + 3]))

    def sums(first, dv, n):
        x = [x_all[layer, HALO + first - 3 + i] for i in range(n + 3)]
        terms = [pairwise([x[i + 3 - k] * dv[i] for i in range(n)]) for k in range(TAPS)]
        return terms + [pairwise(dv[:n])]

    def body(j, carry):
        first = j * step
        dv = list(carry[:3]) + grads(first + 3, step)
        part = sums(first, dv, step)
        back(first, dv, step)
        return tuple(dv[step:step + 3]) + tuple(a + b for a, b in zip(carry[3:], part))

    zero = jnp.zeros((ROWS8, LANES), jnp.float32)
    carry = lax.fori_loop(0, rows // step, body, tuple(grads(0, 3)) + (zero,) * (TAPS + 1))
    for k in range(TAPS + 1):
        g_all[layer * 5 + k] = 0.5 * carry[3 + k]
    extra = 3 * layer
    if extra:
        dv = list(carry[:3]) + grads(rows + 3, extra)
        back(rows, dv, extra)


def fused_kernel(count, layers, rows, channels, scale, owner_ref, x_hbm, c_hbm, w_hbm, b_hbm, q_hbm, l_hbm,
                 out_hbm, p_ref, xh, ch, wv, bv, qv, lv, w_all, x_all, s_all, a_all, g_all, ov,
                 ms, got_m, gs, got_g, part, full_p,
                 load, store, send_h, recv_h, send_m, recv_m, send_g, recv_g, send_p, recv_p):
    here = lax.axis_index("dp")
    width = ROWS8 * LANES
    groups = channels // width
    share = channels // count
    lines = share // LANES
    per = ROWS8 // lines

    def remote(source, target_ref, sent, got, device):
        return pltpu.make_async_remote_copy(
            src_ref=source, dst_ref=target_ref, send_sem=sent, recv_sem=got,
            device_id={"dp": device}, device_id_type=pl.DeviceIdType.MESH)

    locals_ = [
        pltpu.make_async_copy(q_hbm, qv, load.at[0]),
        pltpu.make_async_copy(l_hbm, lv, load.at[1]),
        pltpu.make_async_copy(w_hbm, wv, load.at[2]),
        pltpu.make_async_copy(b_hbm, bv, load.at[3]),
        pltpu.make_async_copy(x_hbm, xh.at[pl.ds(HALO, rows), :], load.at[4]),
        pltpu.make_async_copy(c_hbm, ch.at[pl.ds(0, rows), :], load.at[5]),
    ]
    for copy in locals_:
        copy.start()
    barrier = pltpu.get_barrier_semaphore()

    @pl.loop(1, count)
    def _(step):
        pl.semaphore_signal(barrier, inc=1, device_id={"dp": lax.rem(here + step, count)},
                            device_id_type=pl.DeviceIdType.MESH)

    pl.semaphore_wait(barrier, count - 1)

    def lanes_of(group):
        return pl.ds(pl.multiple_of(group * width, width), width)

    def group_at(device, i):
        return lax.rem(lax.div(device, per) + 1 + i, groups)

    def halo(kind, group, device):
        lanes = lanes_of(group)
        if kind == 0:
            source, target = x_hbm.at[pl.ds(rows - HALO, HALO), lanes], xh.at[pl.ds(0, HALO), lanes]
        elif kind == 1:
            source, target = x_hbm.at[pl.ds(0, HALO), lanes], xh.at[pl.ds(rows + HALO, HALO), lanes]
        else:
            source, target = c_hbm.at[pl.ds(0, HALO), lanes], ch.at[pl.ds(rows, HALO), lanes]
        return remote(source, target, send_h.at[kind, group], recv_h.at[kind, group], device)

    @pl.loop(0, groups)
    def _(i):
        @pl.when(here < count - 1)
        def _():
            halo(0, group_at(here + 1, i), here + 1).start()

        @pl.when(here > 0)
        def _():
            group = group_at(here - 1, i)
            halo(1, group, here - 1).start()
            halo(2, group, here - 1).start()

    @pl.when(here == 0)
    def _():
        xh[pl.ds(0, HALO), :] = jnp.zeros((HALO, channels), jnp.bfloat16)

    @pl.when(here == count - 1)
    def _():
        xh[pl.ds(rows + HALO, HALO), :] = jnp.zeros((HALO, channels), jnp.bfloat16)
        ch[pl.ds(rows, HALO), :] = jnp.zeros((HALO, channels), jnp.bfloat16)

    locals_[0].wait()
    locals_[1].wait()
    damping = 0.1 * jnp.mean(lv[...])

    @pl.loop(0, groups)
    def _(o):
        tile = pl.ds(pl.multiple_of(o * ROWS8, ROWS8), ROWS8)
        inverse = [1.0 / (lv[i, tile, :] + damping) for i in range(5)]
        basis = [[qv[j * 5 + i, tile, :] for i in range(5)] for j in range(5)]
        for at, (j, k) in enumerate(PAIRS):
            value = basis[j][0] * basis[k][0] * inverse[0]
            for i in range(1, 5):
                value = value + basis[j][i] * basis[k][i] * inverse[i]
            for h in range(per):
                ms[o * per + h, at] = value[h * lines:(h + 1) * lines].astype(jnp.bfloat16)

    def send_rows(step):
        target = lax.rem(here + step, count)
        return remote(ms.at[target], got_m.at[step], send_m.at[step], recv_m.at[step], target)

    @pl.loop(1, count)
    def _(step):
        send_rows(step).start()

    got_m[0] = ms[here]
    locals_[2].wait()
    locals_[3].wait()

    @pl.loop(0, channels // LANES)
    def _(g):
        lanes = pl.ds(pl.multiple_of(g * LANES, LANES), LANES)
        for layer in range(layers):
            for k in range(TAPS):
                w_all[layer * TAPS + k, pl.ds(g, 1), :] = wv[layer, pl.ds(k, 1), lanes]
            w_all[layers * TAPS + layer, pl.ds(g, 1), :] = bv[pl.ds(layer, 1), lanes]

    into, back = token_permutation(False), token_permutation(True)
    keep = jnp.where(here > 0, 1.0, 0.0) * jnp.ones((ROWS8, LANES), jnp.float32)
    locals_[4].wait()
    locals_[5].wait()

    def gather_block(ref, at, base):
        return jnp.concatenate(
            [ref[pl.ds(at, HALO), pl.ds(pl.multiple_of(base + g * LANES, LANES), LANES)] for g in range(ROWS8)],
            axis=0)

    def give(group, h):
        owner = group * per + h
        return remote(gs.at[owner], got_g.at[here], send_g.at[owner], recv_g.at[here], owner)

    def written(group):
        return pltpu.make_async_copy(ov.at[:, lanes_of(group)], out_hbm.at[:, lanes_of(group)], store.at[group])

    @pl.loop(0, groups)
    def _(turn):
        group = group_at(here, turn)
        base = group * width
        tile = pl.ds(pl.multiple_of(group * ROWS8, ROWS8), ROWS8)

        @pl.when(here > 0)
        def _():
            halo(0, group, here - 1).wait_recv()

        @pl.when(here < count - 1)
        def _():
            halo(1, group, here + 1).wait_recv()
            halo(2, group, here + 1).wait_recv()

        def arrange(source, target, at):
            pair = jnp.concatenate([gather_block(source, at, base), gather_block(source, at + HALO, base)], axis=1)
            moved = jnp.dot(into, pair, preferred_element_type=jnp.float32)
            target[pl.ds(at, HALO)] = moved[:, :LANES].reshape(HALO, ROWS8, LANES)
            target[pl.ds(at + HALO, HALO)] = moved[:, LANES:].reshape(HALO, ROWS8, LANES)

        @pl.loop(0, (rows + 2 * HALO) // (2 * HALO))
        def _(b):
            arrange(xh, x_all.at[0], pl.multiple_of(b * 2 * HALO, 2 * HALO))

        @pl.loop(0, rows // (2 * HALO))
        def _(b):
            arrange(ch, a_all, pl.multiple_of(b * 2 * HALO, 2 * HALO))

        moved = jnp.dot(into, gather_block(ch, rows, base), preferred_element_type=jnp.float32)
        a_all[pl.ds(rows, HALO)] = moved.reshape(HALO, ROWS8, LANES)

        for layer in range(layers):
            forward_layer(layer, layers, rows, 8, tile, x_all, s_all, w_all, keep)
        for layer in reversed(range(layers)):
            backward_layer(layer, layers, rows, 8, tile, x_all, s_all, a_all, w_all, g_all)

        for h in range(per):
            for term in range(layers * 5):
                gs[group * per + h, term] = g_all[term, h * lines:(h + 1) * lines].astype(jnp.bfloat16)

        for h in range(per):
            @pl.when(group * per + h != here)
            def _():
                give(group, h).start()

        @pl.loop(0, rows // (2 * HALO))
        def _(b):
            at = pl.multiple_of(b * 2 * HALO, 2 * HALO)
            pair = jnp.concatenate(
                [a_all[pl.ds(at, HALO)].reshape(LANES, LANES), a_all[pl.ds(at + HALO, HALO)].reshape(LANES, LANES)],
                axis=1).astype(jnp.bfloat16)
            moved = jnp.dot(back, pair, preferred_element_type=jnp.float32).astype(jnp.bfloat16)
            for g in range(ROWS8):
                lanes = pl.ds(pl.multiple_of(base + g * LANES, LANES), LANES)
                ov[pl.ds(at, HALO), lanes] = moved[g * HALO:(g + 1) * HALO, :LANES]
                ov[pl.ds(at + HALO, HALO), lanes] = moved[g * HALO:(g + 1) * HALO, LANES:]

        written(group).start()

    @pl.loop(1, count)
    def _(step):
        send_rows(step).wait()

    @pl.loop(1, count)
    def _(step):
        source = lax.rem(here + step, count)
        remote(gs.at[source], got_g.at[source], send_g.at[source], recv_g.at[source], source).wait()

    total = gs[here].astype(jnp.float32)
    for step in range(1, count):
        total = total + got_g[lax.rem(here + step, count)].astype(jnp.float32)
    total = total * scale
    order = {pair: i for i, pair in enumerate(PAIRS)}
    for layer in range(layers):
        slot = lax.rem(here - owner_ref[layer] + count, count)
        inverse = got_m[slot].astype(jnp.float32)
        for j in range(5):
            value = None
            for k in range(5):
                term = inverse[order[min(j, k), max(j, k)]] * total[layer * 5 + k]
                value = term if value is None else value + term
            for r in range(lines):
                part[j, pl.ds(layer, 1), r * LANES:(r + 1) * LANES] = value[r:r + 1]

    mine = pl.ds(pl.multiple_of(here * share, share), share)

    def send_part(step):
        return remote(part, full_p.at[:, :, mine], send_p.at[step], recv_p.at[step], lax.rem(here + step, count))

    @pl.loop(1, count)
    def _(step):
        send_part(step).start()

    full_p[:, :, mine] = part[...]

    @pl.loop(0, groups)
    def _(i):
        written(i).wait()

        @pl.when(here < count - 1)
        def _():
            halo(0, i, here + 1).wait_send()

        @pl.when(here > 0)
        def _():
            halo(1, i, here - 1).wait_send()
            halo(2, i, here - 1).wait_send()

    @pl.loop(1, count)
    def _(step):
        send_part(step).wait()

    p_ref[...] = full_p[...]


def fused(acts, cots, weights, bias, owner_map, basis, vals, scale):
    rows, channels = acts.shape
    layers = weights.shape[0]
    count = lax.axis_size("dp")
    share = channels // count
    lines = share // LANES
    groups = channels // (ROWS8 * LANES)
    held = rows + 2 * HALO
    vmem = pl.BlockSpec(memory_space=pltpu.VMEM)
    anywhere = pl.BlockSpec(memory_space=pl.ANY)
    dma = pltpu.SemaphoreType.DMA
    f32, b16 = jnp.float32, jnp.bfloat16
    tall = channels // LANES
    return pl.pallas_call(
        functools.partial(fused_kernel, count, layers, rows, channels, scale),
        out_shape=(
            jax.ShapeDtypeStruct((rows, channels), b16),
            jax.ShapeDtypeStruct((5, layers, channels), f32),
        ),
        in_specs=[pl.BlockSpec(memory_space=pltpu.SMEM)] + [anywhere] * 6,
        out_specs=(anywhere, vmem),
        scratch_shapes=[
            pltpu.VMEM((held, channels), b16),
            pltpu.VMEM((rows + HALO, channels), b16),
            pltpu.VMEM(weights.shape, f32),
            pltpu.VMEM(bias.shape, f32),
            pltpu.VMEM((25, tall, LANES), f32),
            pltpu.VMEM((5, tall, LANES), f32),
            pltpu.VMEM((layers * 5, tall, LANES), f32),
            pltpu.VMEM((layers, held, ROWS8, LANES), f32),
            pltpu.VMEM((layers, held, ROWS8, LANES), f32),
            pltpu.VMEM((rows + HALO, ROWS8, LANES), f32),
            pltpu.VMEM((layers * 5, ROWS8, LANES), f32),
            pltpu.VMEM((rows, channels), b16),
            pltpu.VMEM((count, len(PAIRS), lines, LANES), b16),
            pltpu.VMEM((count, len(PAIRS), lines, LANES), b16),
            pltpu.VMEM((count, layers * 5, lines, LANES), b16),
            pltpu.VMEM((count, layers * 5, lines, LANES), b16),
            pltpu.VMEM((5, layers, share), f32),
            pltpu.VMEM((5, layers, channels), f32),
            dma((6,)), dma((groups,)),
            dma((3, groups)), dma((3, groups)),
            dma((count,)), dma((count,)), dma((count,)), dma((count,)), dma((count,)), dma((count,)),
        ],
        compiler_params=pltpu.CompilerParams(
            collective_id=0, has_side_effects=True, vmem_limit_bytes=48 << 20),
    )(owner_map, acts, cots, weights, bias, basis.reshape(25, tall, LANES), vals.reshape(5, tall, LANES))


def precondition_apart(query_acts, cotangent, conv_weight, conv_bias, owner_map, basis_store, lambda_store,
                       norm_scale):
    rows, channels = query_acts.shape
    layers = conv_weight.shape[0]
    here = lax.axis_index("dp")
    before = shifted(query_acts[rows - HALO_ROWS:], "dp", 1)
    after = shifted(jnp.concatenate([query_acts[:HALO_ROWS], cotangent[:HALO_ROWS]]), "dp", -1)
    halo_acts = jnp.concatenate([before, after[:HALO_ROWS]])
    halo_cots = jnp.concatenate([jnp.zeros_like(before), after[HALO_ROWS:]])
    own_rows = inverse_rows(basis_store[0], lambda_store[0])
    adjoint, partial = window(query_acts, cotangent, halo_acts, halo_cots, conv_weight, conv_bias)
    held = jnp.where((owner_map == here)[:, None, None], own_rows[None], 0.0)
    inverse = lax.psum(held, "dp")
    summed = (lax.psum(partial, "dp") * norm_scale).reshape(layers, 5, channels)
    order = {pair: i for i, pair in enumerate(PAIRS)}
    everyone = jnp.stack([
        sum(inverse[:, order[min(j, k), max(j, k)]] * summed[:, k] for k in range(5))
        for j in range(5)
    ], axis=1)
    return adjoint, everyone


def on_device(query_acts, cotangent, conv_weight, conv_bias, owner_map, basis_store, lambda_store,
              train_grads, batch_index):
    rows, channels = query_acts.shape
    layers = conv_weight.shape[0]
    count = lax.axis_size("dp")
    here = lax.axis_index("dp")
    norm_scale = 1.0 / math.sqrt(rows * count)
    lines = channels // (LANES * count)
    if lines in (4, 8) and channels == lines * LANES * count and rows % (2 * HALO) == 0:
        adjoint, everyone = fused(query_acts, cotangent, conv_weight, conv_bias, owner_map, basis_store[0],
                                  lambda_store[0], norm_scale)
        everyone = everyone.transpose(1, 0, 2)
    else:
        adjoint, everyone = precondition_apart(query_acts, cotangent, conv_weight, conv_bias, owner_map,
                                               basis_store, lambda_store, norm_scale)
    high = everyone.astype(jnp.bfloat16)
    low = (everyone - high.astype(jnp.float32)).astype(jnp.bfloat16)
    both = high.astype(jnp.float32) + low.astype(jnp.float32)
    examples = train_grads.shape[0]
    values = jnp.sum(train_grads.astype(jnp.float32) * both[None], axis=(1, 2, 3))
    values = values * (1.0 / math.sqrt(5 * layers * channels))
    local_index = batch_index - here * examples
    chosen = local_index[:, None] == jnp.arange(examples, dtype=jnp.int32)[None, :]
    scores = jnp.sum(jnp.where(chosen, values[None, :], 0.0), axis=1)
    return (adjoint, scores)


def solution(mesh):
    in_specs = (
        P(("groups", "dp"), None),
        P(("groups", "dp"), None),
        P(),
        P(),
        P(),
        P("dp", None, None),
        P("dp", None, None),
        P(("groups", "dp"), None, None, None),
        P(("groups", "dp")),
    )
    out_specs = (P(("groups", "dp"), None), P(("groups", "dp")))
    return jax.shard_map(
        on_device, mesh=mesh, in_specs=in_specs, out_specs=out_specs, check_vma=False
    )
```

```python
import functools
import math

import jax
import jax.numpy as jnp
import numpy as np
from jax import lax
from jax.experimental import pallas as pl
from jax.experimental.pallas import tpu as pltpu
from jax.sharding import PartitionSpec as P

LANES = 128
SUB = 8
TAPS = 4
HALO_ROWS = 16
PAIRS = [(j, k) for j in range(5) for k in range(j, 5)]


def layout_plan(rows, layers):
    reach = (TAPS - 1) * layers
    extended = rows + 2 * reach
    fold = -(-extended // SUB)
    padded = -(-(fold * SUB) // 16) * 16
    return reach, fold, padded


def permutations(rows, layers):
    reach, fold, padded = layout_plan(rows, layers)
    columns = rows + 2 * HALO_ROWS
    into = np.zeros((padded, columns), np.float32)
    back = np.zeros((rows, padded), np.float32)
    for j in range(fold):
        for s in range(SUB):
            token = fold * s + j - reach
            row = SUB * j + s
            if 0 <= token < rows:
                into[row, token] = 1.0
                back[token, row] = 1.0
            elif -reach <= token < 0:
                into[row, rows + HALO_ROWS + token] = 1.0
            elif rows <= token < rows + reach:
                into[row, HALO_ROWS + token] = 1.0
    return jnp.asarray(into, jnp.bfloat16), jnp.asarray(back, jnp.bfloat16)


def rounded(value):
    return value.astype(jnp.bfloat16).astype(jnp.float32)


def window_chunk(lanes, rows, layers, is_first, w_ref, b_ref, x_all, c_all, slope_all, g_ref):
    reach, fold, padded = layout_plan(rows, layers)
    sub = lax.broadcasted_iota(jnp.int32, (SUB, LANES), 0)
    edges = {}

    def own(j, low, high):
        tokens = [fold * s + j - reach for s in range(SUB)]
        inside = tuple(low <= t < high for t in tokens)
        if all(inside):
            return None
        if inside not in edges:
            lead = next(i for i, ok in enumerate(inside) if ok)
            tail = max(i for i, ok in enumerate(inside) if ok)
            edges[inside] = (sub >= lead) & (sub <= tail)
        return edges[inside]

    zero = jnp.zeros((SUB, LANES), jnp.float32)

    def keep(value, mask):
        return value if mask is None else jnp.where(mask, value, zero)

    def row(ref, *at):
        return jnp.broadcast_to(ref[at[:-1] + (pl.ds(at[-1], 1), lanes)], (SUB, LANES))

    live = {}

    def begun(j):
        mask = own(j, 0, 1 << 30)
        if mask is None:
            return None
        key = id(mask)
        if key not in live:
            live[key] = mask | jnp.logical_not(is_first)
        return live[key]

    last = TAPS - 1
    for layer in range(layers):
        taps = [row(w_ref, layer, k) * 0.5 for k in range(TAPS)]
        bias = row(b_ref, layer) * 0.5
        base = layer * (fold + last) * SUB
        for i in range(last):
            wrapped = x_all[pl.ds(base + (fold + i) * SUB, SUB), lanes]
            x_all[pl.ds(base + i * SUB, SUB), lanes] = pltpu.roll(wrapped, 1, 0)
        x = [x_all[pl.ds(base + i * SUB, SUB), lanes] for i in range(fold + last)]
        following = base + (fold + last + last) * SUB
        for j in range(fold):
            half = bias
            for k in range(TAPS):
                half = half + taps[k] * x[last + j - k]
            bent = jnp.tanh(half)
            up = 1.0 + bent
            slope_all[pl.ds((layer * fold + j) * SUB, SUB), lanes] = up * (1.0 + half * (1.0 - bent))
            if layer < layers - 1:
                fresh = keep(rounded(x[last + j] + half * up), begun(j))
                x_all[pl.ds(following + j * SUB, SUB), lanes] = fresh
    for layer in reversed(range(layers)):
        taps = [row(w_ref, layer, k) * 0.5 for k in range(TAPS)]
        base = layer * (fold + last) * SUB
        doubled = [None] * (fold + last)
        sums = [zero] * (TAPS + 1)

        def at(i):
            return x_all[pl.ds(base + i * SUB, SUB), lanes]

        for j in range(fold):
            adjoint = c_all[pl.ds(j * SUB, SUB), lanes]
            slope = slope_all[pl.ds((layer * fold + j) * SUB, SUB), lanes]
            grad = keep(rounded(adjoint * slope), own(j, 0, 1 << 30))
            doubled[j] = grad
            if j < last:
                doubled[fold + j] = pltpu.roll(grad, SUB - 1, 0)
            inner = keep(grad, own(j, -(1 << 30), rows))
            for k in range(TAPS):
                sums[k] = sums[k] + at(last + j - k) * inner
            sums[TAPS] = sums[TAPS] + inner
        for j in range(fold):
            total = c_all[pl.ds(j * SUB, SUB), lanes]
            back = taps[0] * doubled[j]
            for k in range(1, TAPS):
                back = back + taps[k] * doubled[j + k]
            c_all[pl.ds(j * SUB, SUB), lanes] = rounded(total + back)
        for k in range(TAPS + 1):
            g_ref[pl.ds(layer * 5 + k, 1), lanes] = 0.5 * jnp.sum(sums[k], axis=0, keepdims=True)


def window_kernel(rows, layers, x_ref, c_ref, hx_ref, hc_ref, w_ref, b_ref, into_ref, back_ref,
                  out_ref, g_ref, x_all, c_all, slope_all):
    reach, fold, padded = layout_plan(rows, layers)
    width = x_ref.shape[1]
    is_first = lax.axis_index("dp") == 0
    count = fold * SUB
    acts = jnp.concatenate([x_ref[...], hx_ref[...]], axis=0)
    cots = jnp.concatenate([c_ref[...], hc_ref[...]], axis=0)
    x_all[pl.ds((TAPS - 1) * SUB, count), :] = jnp.dot(
        into_ref[...], acts, preferred_element_type=jnp.float32)[:count]
    c_all[...] = jnp.dot(into_ref[...], cots, preferred_element_type=jnp.float32)

    @pl.loop(0, width // LANES)
    def _(chunk):
        lanes = pl.ds(pl.multiple_of(chunk * LANES, LANES), LANES)
        window_chunk(lanes, rows, layers, is_first, w_ref, b_ref, x_all, c_all, slope_all, g_ref)

    out_ref[...] = jnp.dot(
        back_ref[...], c_all[...].astype(jnp.bfloat16), preferred_element_type=jnp.float32
    ).astype(jnp.bfloat16)


def window(acts, cots, halo_acts, halo_cots, weights, bias):
    rows, channels = acts.shape
    layers = weights.shape[0]
    reach, fold, padded = layout_plan(rows, layers)
    width = 512
    into, back = permutations(rows, layers)
    block = lambda *lead: pl.BlockSpec(lead + (width,), lambda i: (0,) * len(lead) + (i,))
    whole = lambda a: pl.BlockSpec(a.shape, lambda i: (0, 0))
    return pl.pallas_call(
        functools.partial(window_kernel, rows, layers),
        grid=(channels // width,),
        out_shape=(
            jax.ShapeDtypeStruct((rows, channels), jnp.bfloat16),
            jax.ShapeDtypeStruct((layers * 5, channels), jnp.float32),
        ),
        in_specs=[
            block(rows), block(rows), block(2 * HALO_ROWS), block(2 * HALO_ROWS),
            block(layers, TAPS), block(layers), whole(into), whole(back),
        ],
        out_specs=(block(rows), block(layers * 5)),
        scratch_shapes=[
            pltpu.VMEM((layers * (fold + TAPS - 1) * SUB, width), jnp.float32),
            pltpu.VMEM((padded, width), jnp.float32),
            pltpu.VMEM((layers * fold * SUB, width), jnp.float32),
        ],
        compiler_params=pltpu.CompilerParams(vmem_limit_bytes=24 << 20),
        cost_estimate=pl.CostEstimate(flops=200_000_000, bytes_accessed=10_000_000, transcendentals=5_000_000),
    )(acts, cots, halo_acts, halo_cots, weights, bias, into, back)


def shifted(value, axis, steps):
    count = lax.axis_size(axis)
    first, final = (max(0, -steps), min(count, count - steps))
    return lax.ppermute(value, axis, [(s, s + steps) for s in range(first, final)])


def inverse_rows(basis, vals):
    channels = basis.shape[-1]
    blocks = basis.reshape(5, 5, channels)
    scale = 1.0 / (vals + 0.1 * jnp.mean(vals))
    return jnp.stack([jnp.sum(blocks[j] * blocks[k] * scale, axis=0) for j, k in PAIRS])


ROWS8 = 8
HALO = 16


def token_permutation(invert):
    row = lax.broadcasted_iota(jnp.int32, (LANES, LANES), 0)
    col = lax.broadcasted_iota(jnp.int32, (LANES, LANES), 1)
    if invert:
        row, col = col, row
    same = ((row >> 3) == (col & 15)) & ((row & 7) == (col >> 4))
    return jnp.where(same, 1.0, 0.0).astype(jnp.bfloat16)


def forward_layer(layer, layers, rows, step, tile, x_all, s_all, w_all, keep):
    taps = [w_all[layer * TAPS + k, tile, :] * 0.5 for k in range(TAPS)]
    bias = w_all[layers * TAPS + layer, tile, :] * 0.5

    def span(first, n, mask=None):
        x = [x_all[layer, first - 3 + i] for i in range(n + 3)]
        for i in range(n):
            half = ((taps[0] * x[i + 3] + taps[1] * x[i + 2]) + (taps[2] * x[i + 1] + taps[3] * x[i])) + bias
            bent = jnp.tanh(half)
            up = 1.0 + bent
            s_all[layer, first + i] = up * (1.0 + half * (1.0 - bent))
            if layer < layers - 1:
                fresh = x[i + 3] + half * up
                x_all[layer + 1, first + i] = fresh if mask is None else fresh * mask

    early = 3 * (layers - 1 - layer)
    if early:
        span(HALO - early, early, keep)
    total = rows + 3 * layers
    full, rest = total // step, total % step

    @pl.loop(0, full)
    def _(j):
        span(HALO + j * step, step)

    if rest:
        span(HALO + full * step, rest)


def pairwise(values):
    while len(values) > 1:
        values = [values[i] + values[i + 1] if i + 1 < len(values) else values[i]
                  for i in range(0, len(values), 2)]
    return values[0]


def backward_layer(layer, layers, rows, step, tile, x_all, s_all, a_all, w_all, g_all):
    taps = [w_all[layer * TAPS + k, tile, :] * 0.5 for k in range(TAPS)]

    def grads(first, n):
        return [a_all[first + i] * s_all[layer, HALO + first + i] for i in range(n)]

    def back(first, dv, n):
        for i in range(n):
            a_all[first + i] = a_all[first + i] + (
                (taps[0] * dv[i] + taps[1] * dv[i + 1]) + (taps[2] * dv[i + 2] + taps[3] * dv[i + 3]))

    def sums(first, dv, n):
        x = [x_all[layer, HALO + first - 3 + i] for i in range(n + 3)]
        terms = [pairwise([x[i + 3 - k] * dv[i] for i in range(n)]) for k in range(TAPS)]
        return terms + [pairwise(dv[:n])]

    def body(j, carry):
        first = j * step
        dv = list(carry[:3]) + grads(first + 3, step)
        part = sums(first, dv, step)
        back(first, dv, step)
        return tuple(dv[step:step + 3]) + tuple(a + b for a, b in zip(carry[3:], part))

    zero = jnp.zeros((ROWS8, LANES), jnp.float32)
    carry = lax.fori_loop(0, rows // step, body, tuple(grads(0, 3)) + (zero,) * (TAPS + 1))
    for k in range(TAPS + 1):
        g_all[layer * 5 + k] = 0.5 * carry[3 + k]
    extra = 3 * layer
    if extra:
        dv = list(carry[:3]) + grads(rows + 3, extra)
        back(rows, dv, extra)


def fused_kernel(count, layers, rows, channels, scale, final, o_hbm, x_hbm, c_hbm, w_hbm, b_hbm, q_hbm, l_hbm, t_hbm,
                 out_hbm, p_ref, xh, ch, wv, bv, qv, lv, w_all, x_all, s_all, a_all, g_all, ov,
                 ms, got_m, gs, got_g, part, full_p, tv, sacc, owner_ref,
                 load, store, send_h, recv_h, send_m, recv_m, send_g, recv_g, send_p, recv_p):
    here = lax.axis_index("dp")
    width = ROWS8 * LANES
    groups = channels // width
    share = channels // count
    lines = share // LANES
    per = ROWS8 // lines

    def remote(source, target_ref, sent, got, device):
        return pltpu.make_async_remote_copy(
            src_ref=source, dst_ref=target_ref, send_sem=sent, recv_sem=got,
            device_id={"dp": device}, device_id_type=pl.DeviceIdType.MESH)

    locals_ = [
        pltpu.make_async_copy(q_hbm, qv, load.at[0]),
        pltpu.make_async_copy(l_hbm, lv, load.at[1]),
        pltpu.make_async_copy(w_hbm, wv, load.at[2]),
        pltpu.make_async_copy(b_hbm, bv, load.at[3]),
        pltpu.make_async_copy(x_hbm, xh.at[pl.ds(HALO, rows), :], load.at[4]),
        pltpu.make_async_copy(c_hbm, ch.at[pl.ds(0, rows), :], load.at[5]),
        pltpu.make_async_copy(o_hbm, owner_ref, load.at[6]),
        pltpu.make_async_copy(t_hbm, tv, load.at[7]),
    ]
    for copy in locals_:
        copy.start()
    barrier = pltpu.get_barrier_semaphore()

    @pl.loop(1, count)
    def _(step):
        pl.semaphore_signal(barrier, inc=1, device_id={"dp": lax.rem(here + step, count)},
                            device_id_type=pl.DeviceIdType.MESH)

    pl.semaphore_wait(barrier, count - 1)

    def lanes_of(group):
        return pl.ds(pl.multiple_of(group * width, width), width)

    def group_at(device, i):
        return lax.rem(lax.div(device, per) + 1 + i, groups)

    def halo(kind, group, device):
        lanes = lanes_of(group)
        if kind == 0:
            source, target = x_hbm.at[pl.ds(rows - HALO, HALO), lanes], xh.at[pl.ds(0, HALO), lanes]
        elif kind == 1:
            source, target = x_hbm.at[pl.ds(0, HALO), lanes], xh.at[pl.ds(rows + HALO, HALO), lanes]
        else:
            source, target = c_hbm.at[pl.ds(0, HALO), lanes], ch.at[pl.ds(rows, HALO), lanes]
        return remote(source, target, send_h.at[kind, group], recv_h.at[kind, group], device)

    @pl.loop(0, groups)
    def _(i):
        @pl.when(here < count - 1)
        def _():
            halo(0, group_at(here + 1, i), here + 1).start()

        @pl.when(here > 0)
        def _():
            group = group_at(here - 1, i)
            halo(1, group, here - 1).start()
            halo(2, group, here - 1).start()

    @pl.when(here == 0)
    def _():
        xh[pl.ds(0, HALO), :] = jnp.zeros((HALO, channels), jnp.bfloat16)

    @pl.when(here == count - 1)
    def _():
        xh[pl.ds(rows + HALO, HALO), :] = jnp.zeros((HALO, channels), jnp.bfloat16)
        ch[pl.ds(rows, HALO), :] = jnp.zeros((HALO, channels), jnp.bfloat16)

    locals_[0].wait()
    locals_[1].wait()
    damping = 0.1 * jnp.mean(lv[...])

    @pl.loop(0, groups)
    def _(o):
        tile = pl.ds(pl.multiple_of(o * ROWS8, ROWS8), ROWS8)
        inverse = [1.0 / (lv[i, tile, :] + damping) for i in range(5)]
        basis = [[qv[j * 5 + i, tile, :] for i in range(5)] for j in range(5)]
        for at, (j, k) in enumerate(PAIRS):
            value = basis[j][0] * basis[k][0] * inverse[0]
            for i in range(1, 5):
                value = value + basis[j][i] * basis[k][i] * inverse[i]
            for h in range(per):
                ms[o * per + h, at] = value[h * lines:(h + 1) * lines].astype(jnp.bfloat16)

    def send_rows(step):
        target = lax.rem(here + step, count)
        return remote(ms.at[target], got_m.at[step], send_m.at[step], recv_m.at[step], target)

    got_m[0] = ms[here]
    locals_[2].wait()
    locals_[3].wait()

    @pl.loop(0, channels // LANES)
    def _(g):
        lanes = pl.ds(pl.multiple_of(g * LANES, LANES), LANES)
        for layer in range(layers):
            for k in range(TAPS):
                w_all[layer * TAPS + k, pl.ds(g, 1), :] = wv[layer, pl.ds(k, 1), lanes]
            w_all[layers * TAPS + layer, pl.ds(g, 1), :] = bv[pl.ds(layer, 1), lanes]

    into, back = token_permutation(False), token_permutation(True)
    keep = jnp.where(here > 0, 1.0, 0.0) * jnp.ones((ROWS8, LANES), jnp.float32)
    locals_[4].wait()
    locals_[5].wait()

    def gather_block(ref, at, base):
        return jnp.concatenate(
            [ref[pl.ds(at, HALO), pl.ds(pl.multiple_of(base + g * LANES, LANES), LANES)] for g in range(ROWS8)],
            axis=0)

    def give(group, h):
        owner = group * per + h
        return remote(gs.at[owner], got_g.at[here], send_g.at[owner], recv_g.at[here], owner)

    def written(group):
        return pltpu.make_async_copy(ov.at[:, lanes_of(group)], out_hbm.at[:, lanes_of(group)], store.at[group])

    @pl.loop(0, groups)
    def _(turn):
        group = group_at(here, turn)
        base = group * width
        tile = pl.ds(pl.multiple_of(group * ROWS8, ROWS8), ROWS8)

        @pl.when(here > 0)
        def _():
            halo(0, group, here - 1).wait_recv()

        @pl.when(here < count - 1)
        def _():
            halo(1, group, here + 1).wait_recv()
            halo(2, group, here + 1).wait_recv()

        def arrange(source, target, blocks):
            wide = jnp.concatenate([gather_block(source, b * HALO, base) for b in range(blocks)], axis=1)
            moved = jnp.dot(into, wide, preferred_element_type=jnp.float32)
            for b in range(blocks):
                target[pl.ds(b * HALO, HALO)] = moved[:, b * LANES:(b + 1) * LANES].reshape(HALO, ROWS8, LANES)

        arrange(xh, x_all.at[0], rows // HALO + 2)
        arrange(ch, a_all, rows // HALO + 1)

        for layer in range(layers):
            forward_layer(layer, layers, rows, 8, tile, x_all, s_all, w_all, keep)
        for layer in reversed(range(layers)):
            backward_layer(layer, layers, rows, 8, tile, x_all, s_all, a_all, w_all, g_all)

        for h in range(per):
            for term in range(layers * 5):
                gs[group * per + h, term] = g_all[term, h * lines:(h + 1) * lines].astype(jnp.bfloat16)

        for h in range(per):
            @pl.when(group * per + h != here)
            def _():
                give(group, h).start()

        wide = jnp.concatenate(
            [a_all[pl.ds(b * HALO, HALO)].reshape(LANES, LANES).astype(jnp.bfloat16) for b in range(rows // HALO)],
            axis=1)
        moved = jnp.dot(back, wide, preferred_element_type=jnp.float32).astype(jnp.bfloat16)
        for b in range(rows // HALO):
            for g in range(ROWS8):
                lanes = pl.ds(pl.multiple_of(base + g * LANES, LANES), LANES)
                ov[pl.ds(b * HALO, HALO), lanes] = moved[g * HALO:(g + 1) * HALO, b * LANES:(b + 1) * LANES]

        written(group).start()

        @pl.when(turn == 0)
        def _():
            @pl.loop(1, count)
            def _(step):
                send_rows(step).start()

    @pl.loop(1, count)
    def _(step):
        send_rows(step).wait()

    @pl.loop(1, count)
    def _(step):
        source = lax.rem(here + step, count)
        remote(gs.at[source], got_g.at[source], send_g.at[source], recv_g.at[source], source).wait()

    locals_[6].wait()
    total = gs[here].astype(jnp.float32)
    for step in range(1, count):
        total = total + got_g[lax.rem(here + step, count)].astype(jnp.float32)
    total = total * scale
    order = {pair: i for i, pair in enumerate(PAIRS)}
    for layer in range(layers):
        slot = lax.rem(here - owner_ref[layer] + count, count)
        inverse = got_m[slot].astype(jnp.float32)
        for j in range(5):
            value = None
            for k in range(5):
                term = inverse[order[min(j, k), max(j, k)]] * total[layer * 5 + k]
                value = term if value is None else value + term
            for r in range(lines):
                part[j, pl.ds(layer, 1), r * LANES:(r + 1) * LANES] = value[r:r + 1]

    core, side, depth = lax.rem(here, 2), lax.rem(lax.div(here, 2), 2), count // 4
    mate = here + 1 - 2 * core
    across = here + 2 - 4 * side

    def along(device, i):
        return lax.rem(device + 4 * i, count)

    def span_of(owner):
        return pl.ds(pl.multiple_of(owner * share, share), share)

    def pass_on(owner, target, slot):
        lanes = span_of(owner)
        return remote(full_p.at[:, :, lanes], full_p.at[:, :, lanes], send_p.at[slot], recv_p.at[owner], target)

    def score(owner):
        lanes = span_of(owner)
        both = []
        for j in range(5):
            value = full_p[j, :, lanes]
            high = value.astype(jnp.bfloat16).astype(jnp.float32)
            both.append(high + (value - high).astype(jnp.bfloat16).astype(jnp.float32))
        for e in range(tv.shape[0]):
            value = tv[e, 0, :, lanes].astype(jnp.float32) * both[0]
            for j in range(1, 5):
                value = value + tv[e, j, :, lanes].astype(jnp.float32) * both[j]
            sacc[e] = sacc[e] + value

    full_p[:, :, span_of(here)] = part[...]
    sends = []

    def send(owner, target):
        copy = pass_on(owner, target, len(sends))
        copy.start()
        sends.append(copy)

    def await_part(owner):
        pass_on(owner, mate, 0).wait_recv()

    for i in range(1, depth):
        send(here, along(here, i))
    send(here, across)
    send(here, mate)
    sacc[...] = jnp.zeros_like(sacc)
    locals_[7].wait()
    score(here)
    for i in range(1, depth):
        await_part(along(here, i))
        send(along(here, i), across)
        send(along(here, i), mate)
    await_part(across)
    send(across, mate)
    for i in range(1, depth):
        score(along(here, i))
    for i in range(1, depth):
        await_part(along(across, i))
        send(along(across, i), mate)
    for i in range(depth):
        score(along(across, i))
    for owner in (mate, mate + 2 - 4 * side):
        for i in range(depth):
            await_part(along(owner, i))
            score(along(owner, i))

    for e in range(tv.shape[0]):
        rowed = jnp.sum(jnp.sum(sacc[e], axis=0, keepdims=True), axis=1, keepdims=True)
        p_ref[pl.ds(e, 1), :] = jnp.broadcast_to(rowed * final, (1, LANES))

    @pl.loop(0, groups)
    def _(i):
        written(i).wait()

        @pl.when(here < count - 1)
        def _():
            halo(0, i, here + 1).wait_send()

        @pl.when(here > 0)
        def _():
            halo(1, i, here - 1).wait_send()
            halo(2, i, here - 1).wait_send()

    for copy in sends:
        copy.wait_send()


def fused(acts, cots, weights, bias, owner_map, basis, vals, train, scale, final):
    rows, channels = acts.shape
    layers = weights.shape[0]
    count = lax.axis_size("dp")
    share = channels // count
    lines = share // LANES
    groups = channels // (ROWS8 * LANES)
    held = rows + 2 * HALO
    vmem = pl.BlockSpec(memory_space=pltpu.VMEM)
    anywhere = pl.BlockSpec(memory_space=pltpu.HBM)
    dma = pltpu.SemaphoreType.DMA
    f32, b16 = jnp.float32, jnp.bfloat16
    tall = channels // LANES
    return pl.pallas_call(
        functools.partial(fused_kernel, count, layers, rows, channels, scale, final),
        out_shape=(
            jax.ShapeDtypeStruct((rows, channels), b16),
            jax.ShapeDtypeStruct((train.shape[0], LANES), f32),
        ),
        in_specs=[anywhere] * 8,
        out_specs=(anywhere, vmem),
        scratch_shapes=[
            pltpu.VMEM((held, channels), b16),
            pltpu.VMEM((rows + HALO, channels), b16),
            pltpu.VMEM(weights.shape, f32),
            pltpu.VMEM(bias.shape, f32),
            pltpu.VMEM((25, tall, LANES), f32),
            pltpu.VMEM((5, tall, LANES), f32),
            pltpu.VMEM((layers * 5, tall, LANES), f32),
            pltpu.VMEM((layers, held, ROWS8, LANES), f32),
            pltpu.VMEM((layers, held, ROWS8, LANES), f32),
            pltpu.VMEM((rows + HALO, ROWS8, LANES), f32),
            pltpu.VMEM((layers * 5, ROWS8, LANES), f32),
            pltpu.VMEM((rows, channels), b16),
            pltpu.VMEM((count, len(PAIRS), lines, LANES), b16),
            pltpu.VMEM((count, len(PAIRS), lines, LANES), b16),
            pltpu.VMEM((count, layers * 5, lines, LANES), b16),
            pltpu.VMEM((count, layers * 5, lines, LANES), b16),
            pltpu.VMEM((5, layers, share), f32),
            pltpu.VMEM((5, layers, channels), f32),
            pltpu.VMEM(train.shape, b16),
            pltpu.VMEM((train.shape[0], layers, share), f32),
            pltpu.SMEM(owner_map.shape, owner_map.dtype),
            dma((8,)), dma((groups,)),
            dma((3, groups)), dma((3, groups)),
            dma((count,)), dma((count,)), dma((count,)), dma((count,)), dma((count,)), dma((count,)),
        ],
        compiler_params=pltpu.CompilerParams(
            collective_id=0, has_side_effects=True, vmem_limit_bytes=63 << 20),
    )(owner_map, acts, cots, weights, bias, basis.reshape(25, tall, LANES), vals.reshape(5, tall, LANES), train)


def precondition_apart(query_acts, cotangent, conv_weight, conv_bias, owner_map, basis_store, lambda_store,
                       norm_scale):
    rows, channels = query_acts.shape
    layers = conv_weight.shape[0]
    here = lax.axis_index("dp")
    before = shifted(query_acts[rows - HALO_ROWS:], "dp", 1)
    after = shifted(jnp.concatenate([query_acts[:HALO_ROWS], cotangent[:HALO_ROWS]]), "dp", -1)
    halo_acts = jnp.concatenate([before, after[:HALO_ROWS]])
    halo_cots = jnp.concatenate([jnp.zeros_like(before), after[HALO_ROWS:]])
    own_rows = inverse_rows(basis_store[0], lambda_store[0])
    adjoint, partial = window(query_acts, cotangent, halo_acts, halo_cots, conv_weight, conv_bias)
    held = jnp.where((owner_map == here)[:, None, None], own_rows[None], 0.0)
    inverse = lax.psum(held, "dp")
    summed = (lax.psum(partial, "dp") * norm_scale).reshape(layers, 5, channels)
    order = {pair: i for i, pair in enumerate(PAIRS)}
    everyone = jnp.stack([
        sum(inverse[:, order[min(j, k), max(j, k)]] * summed[:, k] for k in range(5))
        for j in range(5)
    ], axis=1)
    return adjoint, everyone


def on_device(query_acts, cotangent, conv_weight, conv_bias, owner_map, basis_store, lambda_store,
              train_grads, batch_index):
    rows, channels = query_acts.shape
    layers = conv_weight.shape[0]
    count = lax.axis_size("dp")
    here = lax.axis_index("dp")
    norm_scale = 1.0 / math.sqrt(rows * count)
    lines = channels // (LANES * count)
    examples = train_grads.shape[0]
    final = 1.0 / math.sqrt(5 * layers * channels)
    if lines in (4, 8) and count % 4 == 0 and channels == lines * LANES * count and rows % HALO == 0:
        adjoint, values = fused(query_acts, cotangent, conv_weight, conv_bias, owner_map, basis_store[0],
                                lambda_store[0], train_grads.transpose(0, 2, 1, 3), norm_scale, final)
        values = values[:, 0]
    else:
        adjoint, everyone = precondition_apart(query_acts, cotangent, conv_weight, conv_bias, owner_map,
                                               basis_store, lambda_store, norm_scale)
        high = everyone.astype(jnp.bfloat16)
        low = (everyone - high.astype(jnp.float32)).astype(jnp.bfloat16)
        both = high.astype(jnp.float32) + low.astype(jnp.float32)
        values = jnp.sum(train_grads.astype(jnp.float32) * both[None], axis=(1, 2, 3)) * final
    local_index = batch_index - here * examples
    chosen = local_index[:, None] == jnp.arange(examples, dtype=jnp.int32)[None, :]
    scores = jnp.sum(jnp.where(chosen, values[None, :], 0.0), axis=1)
    return (adjoint, scores)


def solution(mesh):
    in_specs = (
        P(("groups", "dp"), None),
        P(("groups", "dp"), None),
        P(),
        P(),
        P(),
        P("dp", None, None),
        P("dp", None, None),
        P(("groups", "dp"), None, None, None),
        P(("groups", "dp")),
    )
    out_specs = (P(("groups", "dp"), None), P(("groups", "dp")))
    return jax.shard_map(
        on_device, mesh=mesh, in_specs=in_specs, out_specs=out_specs, check_vma=False
    )
```

```python
import functools
import math

import jax
import jax.numpy as jnp
import numpy as np
from jax import lax
from jax.experimental import pallas as pl
from jax.experimental.pallas import tpu as pltpu
from jax.sharding import PartitionSpec as P

LANES = 128
SUB = 8
TAPS = 4
HALO_ROWS = 16
PAIRS = [(j, k) for j in range(5) for k in range(j, 5)]


def layout_plan(rows, layers):
    reach = (TAPS - 1) * layers
    extended = rows + 2 * reach
    fold = -(-extended // SUB)
    padded = -(-(fold * SUB) // 16) * 16
    return reach, fold, padded


def permutations(rows, layers):
    reach, fold, padded = layout_plan(rows, layers)
    columns = rows + 2 * HALO_ROWS
    into = np.zeros((padded, columns), np.float32)
    back = np.zeros((rows, padded), np.float32)
    for j in range(fold):
        for s in range(SUB):
            token = fold * s + j - reach
            row = SUB * j + s
            if 0 <= token < rows:
                into[row, token] = 1.0
                back[token, row] = 1.0
            elif -reach <= token < 0:
                into[row, rows + HALO_ROWS + token] = 1.0
            elif rows <= token < rows + reach:
                into[row, HALO_ROWS + token] = 1.0
    return jnp.asarray(into, jnp.bfloat16), jnp.asarray(back, jnp.bfloat16)


def rounded(value):
    return value.astype(jnp.bfloat16).astype(jnp.float32)


def window_chunk(lanes, rows, layers, is_first, w_ref, b_ref, x_all, c_all, slope_all, g_ref):
    reach, fold, padded = layout_plan(rows, layers)
    sub = lax.broadcasted_iota(jnp.int32, (SUB, LANES), 0)
    edges = {}

    def own(j, low, high):
        tokens = [fold * s + j - reach for s in range(SUB)]
        inside = tuple(low <= t < high for t in tokens)
        if all(inside):
            return None
        if inside not in edges:
            lead = next(i for i, ok in enumerate(inside) if ok)
            tail = max(i for i, ok in enumerate(inside) if ok)
            edges[inside] = (sub >= lead) & (sub <= tail)
        return edges[inside]

    zero = jnp.zeros((SUB, LANES), jnp.float32)

    def keep(value, mask):
        return value if mask is None else jnp.where(mask, value, zero)

    def row(ref, *at):
        return jnp.broadcast_to(ref[at[:-1] + (pl.ds(at[-1], 1), lanes)], (SUB, LANES))

    live = {}

    def begun(j):
        mask = own(j, 0, 1 << 30)
        if mask is None:
            return None
        key = id(mask)
        if key not in live:
            live[key] = mask | jnp.logical_not(is_first)
        return live[key]

    last = TAPS - 1
    for layer in range(layers):
        taps = [row(w_ref, layer, k) * 0.5 for k in range(TAPS)]
        bias = row(b_ref, layer) * 0.5
        base = layer * (fold + last) * SUB
        for i in range(last):
            wrapped = x_all[pl.ds(base + (fold + i) * SUB, SUB), lanes]
            x_all[pl.ds(base + i * SUB, SUB), lanes] = pltpu.roll(wrapped, 1, 0)
        x = [x_all[pl.ds(base + i * SUB, SUB), lanes] for i in range(fold + last)]
        following = base + (fold + last + last) * SUB
        for j in range(fold):
            half = bias
            for k in range(TAPS):
                half = half + taps[k] * x[last + j - k]
            bent = jnp.tanh(half)
            up = 1.0 + bent
            slope_all[pl.ds((layer * fold + j) * SUB, SUB), lanes] = up * (1.0 + half * (1.0 - bent))
            if layer < layers - 1:
                fresh = keep(rounded(x[last + j] + half * up), begun(j))
                x_all[pl.ds(following + j * SUB, SUB), lanes] = fresh
    for layer in reversed(range(layers)):
        taps = [row(w_ref, layer, k) * 0.5 for k in range(TAPS)]
        base = layer * (fold + last) * SUB
        doubled = [None] * (fold + last)
        sums = [zero] * (TAPS + 1)

        def at(i):
            return x_all[pl.ds(base + i * SUB, SUB), lanes]

        for j in range(fold):
            adjoint = c_all[pl.ds(j * SUB, SUB), lanes]
            slope = slope_all[pl.ds((layer * fold + j) * SUB, SUB), lanes]
            grad = keep(rounded(adjoint * slope), own(j, 0, 1 << 30))
            doubled[j] = grad
            if j < last:
                doubled[fold + j] = pltpu.roll(grad, SUB - 1, 0)
            inner = keep(grad, own(j, -(1 << 30), rows))
            for k in range(TAPS):
                sums[k] = sums[k] + at(last + j - k) * inner
            sums[TAPS] = sums[TAPS] + inner
        for j in range(fold):
            total = c_all[pl.ds(j * SUB, SUB), lanes]
            back = taps[0] * doubled[j]
            for k in range(1, TAPS):
                back = back + taps[k] * doubled[j + k]
            c_all[pl.ds(j * SUB, SUB), lanes] = rounded(total + back)
        for k in range(TAPS + 1):
            g_ref[pl.ds(layer * 5 + k, 1), lanes] = 0.5 * jnp.sum(sums[k], axis=0, keepdims=True)


def window_kernel(rows, layers, x_ref, c_ref, hx_ref, hc_ref, w_ref, b_ref, into_ref, back_ref,
                  out_ref, g_ref, x_all, c_all, slope_all):
    reach, fold, padded = layout_plan(rows, layers)
    width = x_ref.shape[1]
    is_first = lax.axis_index("dp") == 0
    count = fold * SUB
    acts = jnp.concatenate([x_ref[...], hx_ref[...]], axis=0)
    cots = jnp.concatenate([c_ref[...], hc_ref[...]], axis=0)
    x_all[pl.ds((TAPS - 1) * SUB, count), :] = jnp.dot(
        into_ref[...], acts, preferred_element_type=jnp.float32)[:count]
    c_all[...] = jnp.dot(into_ref[...], cots, preferred_element_type=jnp.float32)

    @pl.loop(0, width // LANES)
    def _(chunk):
        lanes = pl.ds(pl.multiple_of(chunk * LANES, LANES), LANES)
        window_chunk(lanes, rows, layers, is_first, w_ref, b_ref, x_all, c_all, slope_all, g_ref)

    out_ref[...] = jnp.dot(
        back_ref[...], c_all[...].astype(jnp.bfloat16), preferred_element_type=jnp.float32
    ).astype(jnp.bfloat16)


def window(acts, cots, halo_acts, halo_cots, weights, bias):
    rows, channels = acts.shape
    layers = weights.shape[0]
    reach, fold, padded = layout_plan(rows, layers)
    width = 512
    into, back = permutations(rows, layers)
    block = lambda *lead: pl.BlockSpec(lead + (width,), lambda i: (0,) * len(lead) + (i,))
    whole = lambda a: pl.BlockSpec(a.shape, lambda i: (0, 0))
    return pl.pallas_call(
        functools.partial(window_kernel, rows, layers),
        grid=(channels // width,),
        out_shape=(
            jax.ShapeDtypeStruct((rows, channels), jnp.bfloat16),
            jax.ShapeDtypeStruct((layers * 5, channels), jnp.float32),
        ),
        in_specs=[
            block(rows), block(rows), block(2 * HALO_ROWS), block(2 * HALO_ROWS),
            block(layers, TAPS), block(layers), whole(into), whole(back),
        ],
        out_specs=(block(rows), block(layers * 5)),
        scratch_shapes=[
            pltpu.VMEM((layers * (fold + TAPS - 1) * SUB, width), jnp.float32),
            pltpu.VMEM((padded, width), jnp.float32),
            pltpu.VMEM((layers * fold * SUB, width), jnp.float32),
        ],
        compiler_params=pltpu.CompilerParams(vmem_limit_bytes=24 << 20),
        cost_estimate=pl.CostEstimate(flops=200_000_000, bytes_accessed=10_000_000, transcendentals=5_000_000),
    )(acts, cots, halo_acts, halo_cots, weights, bias, into, back)


def shifted(value, axis, steps):
    count = lax.axis_size(axis)
    first, final = (max(0, -steps), min(count, count - steps))
    return lax.ppermute(value, axis, [(s, s + steps) for s in range(first, final)])


def inverse_rows(basis, vals):
    channels = basis.shape[-1]
    blocks = basis.reshape(5, 5, channels)
    scale = 1.0 / (vals + 0.1 * jnp.mean(vals))
    return jnp.stack([jnp.sum(blocks[j] * blocks[k] * scale, axis=0) for j, k in PAIRS])


ROWS8 = 8
HALO = 16


def token_permutation(invert):
    row = lax.broadcasted_iota(jnp.int32, (LANES, LANES), 0)
    col = lax.broadcasted_iota(jnp.int32, (LANES, LANES), 1)
    if invert:
        row, col = col, row
    same = ((row >> 3) == (col & 15)) & ((row & 7) == (col >> 4))
    return jnp.where(same, 1.0, 0.0).astype(jnp.bfloat16)


def forward_layer(layer, layers, rows, step, tile, x_all, s_all, w_all, keep):
    taps = [w_all[layer * TAPS + k, tile, :] * 0.5 for k in range(TAPS)]
    bias = w_all[layers * TAPS + layer, tile, :] * 0.5

    def span(first, n, mask=None):
        x = [x_all[layer, first - 3 + i] for i in range(n + 3)]
        for i in range(n):
            half = ((taps[0] * x[i + 3] + taps[1] * x[i + 2]) + (taps[2] * x[i + 1] + taps[3] * x[i])) + bias
            bent = jnp.tanh(half)
            up = 1.0 + bent
            gain = half * up
            s_all[layer, first + i] = up + gain * (1.0 - bent)
            if layer < layers - 1:
                fresh = x[i + 3] + gain
                x_all[layer + 1, first + i] = fresh if mask is None else fresh * mask

    early = 3 * (layers - 1 - layer)
    if early:
        span(HALO - early, early, keep)
    total = rows + 3 * layers
    full, rest = total // step, total % step

    @pl.loop(0, full)
    def _(j):
        span(HALO + j * step, step)

    if rest:
        span(HALO + full * step, rest)


def pairwise(values):
    while len(values) > 1:
        values = [values[i] + values[i + 1] if i + 1 < len(values) else values[i]
                  for i in range(0, len(values), 2)]
    return values[0]


def backward_layer(layer, layers, rows, step, tile, x_all, s_all, a_all, w_all, g_all):
    taps = [w_all[layer * TAPS + k, tile, :] * 0.5 for k in range(TAPS)]

    def grads(first, n):
        return [a_all[first + i] * s_all[layer, HALO + first + i] for i in range(n)]

    def back(first, dv, n):
        for i in range(n):
            a_all[first + i] = a_all[first + i] + (
                (taps[0] * dv[i] + taps[1] * dv[i + 1]) + (taps[2] * dv[i + 2] + taps[3] * dv[i + 3]))

    def sums(first, dv, n):
        x = [x_all[layer, HALO + first - 3 + i] for i in range(n + 3)]
        terms = [pairwise([x[i + 3 - k] * dv[i] for i in range(n)]) for k in range(TAPS)]
        return terms + [pairwise(dv[:n])]

    def body(j, carry):
        first = j * step
        dv = list(carry[:3]) + grads(first + 3, step)
        part = sums(first, dv, step)
        back(first, dv, step)
        return tuple(dv[step:step + 3]) + tuple(a + b for a, b in zip(carry[3:], part))

    zero = jnp.zeros((ROWS8, LANES), jnp.float32)
    carry = lax.fori_loop(0, rows // step, body, tuple(grads(0, 3)) + (zero,) * (TAPS + 1))
    for k in range(TAPS + 1):
        g_all[layer * 5 + k] = 0.5 * carry[3 + k]
    extra = 3 * layer
    if extra:
        dv = list(carry[:3]) + grads(rows + 3, extra)
        back(rows, dv, extra)


def fused_kernel(count, layers, rows, channels, scale, final, o_hbm, x_hbm, c_hbm, w_hbm, b_hbm, q_hbm, l_hbm, t_hbm,
                 out_hbm, p_ref, xh, ch, wv, bv, qv, lv, w_all, x_all, s_all, a_all, g_all, ov,
                 ms, got_m, gs, got_g, part, full_p, tv, sacc, owner_ref,
                 load, store, send_h, recv_h, send_m, recv_m, send_g, recv_g, send_p, recv_p):
    here = lax.axis_index("dp")
    width = ROWS8 * LANES
    groups = channels // width
    share = channels // count
    lines = share // LANES
    per = ROWS8 // lines

    def remote(source, target_ref, sent, got, device):
        return pltpu.make_async_remote_copy(
            src_ref=source, dst_ref=target_ref, send_sem=sent, recv_sem=got,
            device_id={"dp": device}, device_id_type=pl.DeviceIdType.MESH)

    locals_ = [
        pltpu.make_async_copy(q_hbm, qv, load.at[0]),
        pltpu.make_async_copy(l_hbm, lv, load.at[1]),
        pltpu.make_async_copy(w_hbm, wv, load.at[2]),
        pltpu.make_async_copy(b_hbm, bv, load.at[3]),
        pltpu.make_async_copy(x_hbm, xh.at[pl.ds(HALO, rows), :], load.at[4]),
        pltpu.make_async_copy(c_hbm, ch.at[pl.ds(0, rows), :], load.at[5]),
        pltpu.make_async_copy(o_hbm, owner_ref, load.at[6]),
        pltpu.make_async_copy(t_hbm, tv, load.at[7]),
    ]
    for copy in locals_:
        copy.start()
    barrier = pltpu.get_barrier_semaphore()

    @pl.loop(1, count)
    def _(step):
        pl.semaphore_signal(barrier, inc=1, device_id={"dp": lax.rem(here + step, count)},
                            device_id_type=pl.DeviceIdType.MESH)

    pl.semaphore_wait(barrier, count - 1)

    def lanes_of(group):
        return pl.ds(pl.multiple_of(group * width, width), width)

    def group_at(device, i):
        return lax.rem(lax.div(device, per) + 1 + i, groups)

    def halo(kind, group, device):
        lanes = lanes_of(group)
        if kind == 0:
            source, target = x_hbm.at[pl.ds(rows - HALO, HALO), lanes], xh.at[pl.ds(0, HALO), lanes]
        elif kind == 1:
            source, target = x_hbm.at[pl.ds(0, HALO), lanes], xh.at[pl.ds(rows + HALO, HALO), lanes]
        else:
            source, target = c_hbm.at[pl.ds(0, HALO), lanes], ch.at[pl.ds(rows, HALO), lanes]
        return remote(source, target, send_h.at[kind, group], recv_h.at[kind, group], device)

    def send_halos(turn):
        @pl.when(here < count - 1)
        def _():
            halo(0, group_at(here + 1, turn), here + 1).start()

        @pl.when(here > 0)
        def _():
            group = group_at(here - 1, turn)
            halo(1, group, here - 1).start()
            halo(2, group, here - 1).start()

    ahead = 2
    for turn in range(ahead):
        send_halos(turn)

    @pl.when(here == 0)
    def _():
        xh[pl.ds(0, HALO), :] = jnp.zeros((HALO, channels), jnp.bfloat16)

    @pl.when(here == count - 1)
    def _():
        xh[pl.ds(rows + HALO, HALO), :] = jnp.zeros((HALO, channels), jnp.bfloat16)
        ch[pl.ds(rows, HALO), :] = jnp.zeros((HALO, channels), jnp.bfloat16)

    locals_[0].wait()
    locals_[1].wait()
    damping = 0.1 * jnp.mean(lv[...])

    @pl.loop(0, groups)
    def _(o):
        tile = pl.ds(pl.multiple_of(o * ROWS8, ROWS8), ROWS8)
        inverse = [1.0 / (lv[i, tile, :] + damping) for i in range(5)]
        basis = [[qv[j * 5 + i, tile, :] for i in range(5)] for j in range(5)]
        for at, (j, k) in enumerate(PAIRS):
            value = basis[j][0] * basis[k][0] * inverse[0]
            for i in range(1, 5):
                value = value + basis[j][i] * basis[k][i] * inverse[i]
            for h in range(per):
                ms[o * per + h, at] = value[h * lines:(h + 1) * lines].astype(jnp.bfloat16)

    def send_rows(step):
        target = lax.rem(here + step, count)
        return remote(ms.at[target], got_m.at[step], send_m.at[step], recv_m.at[step], target)

    got_m[0] = ms[here]
    locals_[2].wait()
    locals_[3].wait()

    @pl.loop(0, channels // LANES)
    def _(g):
        lanes = pl.ds(pl.multiple_of(g * LANES, LANES), LANES)
        for layer in range(layers):
            for k in range(TAPS):
                w_all[layer * TAPS + k, pl.ds(g, 1), :] = wv[layer, pl.ds(k, 1), lanes]
            w_all[layers * TAPS + layer, pl.ds(g, 1), :] = bv[pl.ds(layer, 1), lanes]

    into = token_permutation(False)
    keep = jnp.where(here > 0, 1.0, 0.0) * jnp.ones((ROWS8, LANES), jnp.float32)
    locals_[4].wait()
    locals_[5].wait()

    def gather_block(ref, at, base):
        return jnp.concatenate(
            [ref[pl.ds(at, HALO), pl.ds(pl.multiple_of(base + g * LANES, LANES), LANES)] for g in range(ROWS8)],
            axis=0)

    def give(group, h):
        owner = group * per + h
        return remote(gs.at[owner], got_g.at[here], send_g.at[owner], recv_g.at[here], owner)

    def written(group):
        return pltpu.make_async_copy(ov.at[group], out_hbm.at[group], store.at[group])

    @pl.loop(0, groups)
    def _(turn):
        group = group_at(here, turn)
        base = group * width
        tile = pl.ds(pl.multiple_of(group * ROWS8, ROWS8), ROWS8)

        @pl.when(turn < groups - ahead)
        def _():
            send_halos(turn + ahead)

        @pl.when(here > 0)
        def _():
            halo(0, group, here - 1).wait_recv()

        @pl.when(here < count - 1)
        def _():
            halo(1, group, here + 1).wait_recv()
            halo(2, group, here + 1).wait_recv()

        def arrange(source, target, blocks):
            wide = jnp.concatenate([gather_block(source, b * HALO, base) for b in range(blocks)], axis=1)
            moved = jnp.dot(into, wide, preferred_element_type=jnp.float32)
            for b in range(blocks):
                target[pl.ds(b * HALO, HALO)] = moved[:, b * LANES:(b + 1) * LANES].reshape(HALO, ROWS8, LANES)

        arrange(xh, x_all.at[0], rows // HALO + 2)
        arrange(ch, a_all, rows // HALO + 1)

        for layer in range(layers):
            forward_layer(layer, layers, rows, 8, tile, x_all, s_all, w_all, keep)
        for layer in reversed(range(layers)):
            backward_layer(layer, layers, rows, 8, tile, x_all, s_all, a_all, w_all, g_all)

        for h in range(per):
            for term in range(layers * 5):
                gs[group * per + h, term] = g_all[term, h * lines:(h + 1) * lines].astype(jnp.bfloat16)

        for h in range(per):
            @pl.when(group * per + h != here)
            def _():
                give(group, h).start()

        ov[group] = a_all[pl.ds(0, rows)].reshape(rows * ROWS8, LANES).astype(jnp.bfloat16)
        written(group).start()

        @pl.when(turn == 0)
        def _():
            @pl.loop(1, count)
            def _(step):
                send_rows(step).start()

    @pl.loop(1, count)
    def _(step):
        send_rows(step).wait()

    @pl.loop(1, count)
    def _(step):
        source = lax.rem(here + step, count)
        remote(gs.at[source], got_g.at[source], send_g.at[source], recv_g.at[source], source).wait()

    locals_[6].wait()
    total = gs[here].astype(jnp.float32)
    for step in range(1, count):
        total = total + got_g[lax.rem(here + step, count)].astype(jnp.float32)
    total = total * scale
    order = {pair: i for i, pair in enumerate(PAIRS)}
    for layer in range(layers):
        slot = lax.rem(here - owner_ref[layer] + count, count)
        inverse = got_m[slot].astype(jnp.float32)
        for j in range(5):
            value = None
            for k in range(5):
                term = inverse[order[min(j, k), max(j, k)]] * total[layer * 5 + k]
                value = term if value is None else value + term
            for r in range(lines):
                part[j, pl.ds(layer, 1), r * LANES:(r + 1) * LANES] = value[r:r + 1]

    core, side, depth = lax.rem(here, 2), lax.rem(lax.div(here, 2), 2), count // 4
    mate = here + 1 - 2 * core
    across = here + 2 - 4 * side

    def along(device, i):
        return lax.rem(device + 4 * i, count)

    def span_of(owner):
        return pl.ds(pl.multiple_of(owner * share, share), share)

    def pass_on(owner, target, slot):
        lanes = span_of(owner)
        return remote(full_p.at[:, :, lanes], full_p.at[:, :, lanes], send_p.at[slot], recv_p.at[owner], target)

    def score(owner):
        lanes = span_of(owner)
        both = []
        for j in range(5):
            value = full_p[j, :, lanes]
            high = value.astype(jnp.bfloat16).astype(jnp.float32)
            both.append(high + (value - high).astype(jnp.bfloat16).astype(jnp.float32))
        for e in range(tv.shape[0]):
            value = tv[e, 0, :, lanes].astype(jnp.float32) * both[0]
            for j in range(1, 5):
                value = value + tv[e, j, :, lanes].astype(jnp.float32) * both[j]
            sacc[e] = sacc[e] + value

    full_p[:, :, span_of(here)] = part[...]
    sends = []

    def send(owner, target):
        copy = pass_on(owner, target, len(sends))
        copy.start()
        sends.append(copy)

    def await_part(owner):
        pass_on(owner, mate, 0).wait_recv()

    for i in range(1, depth):
        send(here, along(here, i))
    send(here, across)
    send(here, mate)
    sacc[...] = jnp.zeros_like(sacc)
    locals_[7].wait()
    score(here)
    for i in range(1, depth):
        await_part(along(here, i))
        send(along(here, i), across)
        send(along(here, i), mate)
    await_part(across)
    send(across, mate)
    for i in range(1, depth):
        score(along(here, i))
    for i in range(1, depth):
        await_part(along(across, i))
        send(along(across, i), mate)
    for i in range(depth):
        score(along(across, i))
    for owner in (mate, mate + 2 - 4 * side):
        for i in range(depth):
            await_part(along(owner, i))
            score(along(owner, i))

    for e in range(tv.shape[0]):
        rowed = jnp.sum(jnp.sum(sacc[e], axis=0, keepdims=True), axis=1, keepdims=True)
        p_ref[pl.ds(e, 1), :] = jnp.broadcast_to(rowed * final, (1, LANES))

    @pl.loop(0, groups)
    def _(i):
        written(i).wait()

        @pl.when(here < count - 1)
        def _():
            halo(0, i, here + 1).wait_send()

        @pl.when(here > 0)
        def _():
            halo(1, i, here - 1).wait_send()
            halo(2, i, here - 1).wait_send()

    for copy in sends:
        copy.wait_send()


def fused(acts, cots, weights, bias, owner_map, basis, vals, train, scale, final):
    rows, channels = acts.shape
    layers = weights.shape[0]
    count = lax.axis_size("dp")
    share = channels // count
    lines = share // LANES
    groups = channels // (ROWS8 * LANES)
    held = rows + 2 * HALO
    vmem = pl.BlockSpec(memory_space=pltpu.VMEM)
    anywhere = pl.BlockSpec(memory_space=pltpu.HBM)
    dma = pltpu.SemaphoreType.DMA
    f32, b16 = jnp.float32, jnp.bfloat16
    tall = channels // LANES
    return pl.pallas_call(
        functools.partial(fused_kernel, count, layers, rows, channels, scale, final),
        out_shape=(
            jax.ShapeDtypeStruct((groups, rows * ROWS8, LANES), b16),
            jax.ShapeDtypeStruct((train.shape[0], LANES), f32),
        ),
        in_specs=[anywhere] * 8,
        out_specs=(anywhere, vmem),
        scratch_shapes=[
            pltpu.VMEM((held, channels), b16),
            pltpu.VMEM((rows + HALO, channels), b16),
            pltpu.VMEM(weights.shape, f32),
            pltpu.VMEM(bias.shape, f32),
            pltpu.VMEM((25, tall, LANES), f32),
            pltpu.VMEM((5, tall, LANES), f32),
            pltpu.VMEM((layers * 5, tall, LANES), f32),
            pltpu.VMEM((layers, held, ROWS8, LANES), f32),
            pltpu.VMEM((layers, held, ROWS8, LANES), f32),
            pltpu.VMEM((rows + HALO, ROWS8, LANES), f32),
            pltpu.VMEM((layers * 5, ROWS8, LANES), f32),
            pltpu.VMEM((groups, rows * ROWS8, LANES), b16),
            pltpu.VMEM((count, len(PAIRS), lines, LANES), b16),
            pltpu.VMEM((count, len(PAIRS), lines, LANES), b16),
            pltpu.VMEM((count, layers * 5, lines, LANES), b16),
            pltpu.VMEM((count, layers * 5, lines, LANES), b16),
            pltpu.VMEM((5, layers, share), f32),
            pltpu.VMEM((5, layers, channels), f32),
            pltpu.VMEM(train.shape, b16),
            pltpu.VMEM((train.shape[0], layers, share), f32),
            pltpu.SMEM(owner_map.shape, owner_map.dtype),
            dma((8,)), dma((groups,)),
            dma((3, groups)), dma((3, groups)),
            dma((count,)), dma((count,)), dma((count,)), dma((count,)), dma((count,)), dma((count,)),
        ],
        compiler_params=pltpu.CompilerParams(
            collective_id=0, has_side_effects=True, vmem_limit_bytes=63 << 20),
    )(owner_map, acts, cots, weights, bias, basis.reshape(25, tall, LANES), vals.reshape(5, tall, LANES), train)


def finish_kernel(rows, a_hbm, v_hbm, i_hbm, out_hbm, s_hbm, av, ov, v_ref, i_ref, s_ref, load, store):
    back = token_permutation(True)
    blocks = rows // HALO
    groups = a_hbm.shape[0]
    width = ROWS8 * LANES

    def read(i):
        return pltpu.make_async_copy(a_hbm.at[i], av.at[i], load.at[i])

    def write(i):
        lanes = pl.ds(i * width, width)
        return pltpu.make_async_copy(ov.at[:, lanes], out_hbm.at[:, lanes], store.at[i])

    for i in range(groups):
        read(i).start()
    small = [pltpu.make_async_copy(v_hbm, v_ref, load.at[groups]),
             pltpu.make_async_copy(i_hbm, i_ref, load.at[groups + 1])]
    picked = pltpu.make_async_copy(s_ref, s_hbm, store.at[groups])
    for copy in small:
        copy.start()
    examples = v_ref.shape[0]
    picks = i_ref.shape[1]
    for i in range(groups):
        read(i).wait()
        wide = jnp.concatenate([av[i, pl.ds(b * LANES, LANES), :] for b in range(blocks)], axis=1)
        moved = jnp.dot(back, wide, preferred_element_type=jnp.float32).astype(jnp.bfloat16)
        for b in range(blocks):
            for g in range(ROWS8):
                ov[pl.ds(b * HALO, HALO), pl.ds(i * width + g * LANES, LANES)] = (
                    moved[g * HALO:(g + 1) * HALO, b * LANES:(b + 1) * LANES])
        write(i).start()
        if i == 0:
            for copy in small:
                copy.wait()
            local = i_ref[...] - lax.axis_index("dp") * examples
            chosen = jnp.broadcast_to(local, (examples, picks)) == lax.broadcasted_iota(jnp.int32, (examples, picks), 0)
            s_ref[...] = jnp.sum(jnp.where(chosen, v_ref[:, :picks], 0.0), axis=0, keepdims=True)
            picked.start()
    for i in range(groups):
        write(i).wait()
    picked.wait()


def finish(moved, values, batch_index, rows):
    groups = moved.shape[0]
    picks = batch_index.shape[0]
    channels = groups * ROWS8 * LANES
    anywhere = pl.BlockSpec(memory_space=pltpu.HBM)
    return pl.pallas_call(
        functools.partial(finish_kernel, rows),
        out_shape=(
            jax.ShapeDtypeStruct((rows, channels), jnp.bfloat16),
            jax.ShapeDtypeStruct((1, picks), jnp.float32),
        ),
        in_specs=[anywhere] * 3,
        out_specs=(anywhere, anywhere),
        scratch_shapes=[
            pltpu.VMEM(moved.shape, moved.dtype),
            pltpu.VMEM((rows, channels), moved.dtype),
            pltpu.VMEM(values.shape, values.dtype),
            pltpu.VMEM((1, picks), batch_index.dtype),
            pltpu.VMEM((1, picks), jnp.float32),
            pltpu.SemaphoreType.DMA((groups + 2,)),
            pltpu.SemaphoreType.DMA((groups + 1,)),
        ],
        compiler_params=pltpu.CompilerParams(vmem_limit_bytes=63 << 20),
    )(moved, values, batch_index.reshape(1, picks))


def precondition_apart(query_acts, cotangent, conv_weight, conv_bias, owner_map, basis_store, lambda_store,
                       norm_scale):
    rows, channels = query_acts.shape
    layers = conv_weight.shape[0]
    here = lax.axis_index("dp")
    before = shifted(query_acts[rows - HALO_ROWS:], "dp", 1)
    after = shifted(jnp.concatenate([query_acts[:HALO_ROWS], cotangent[:HALO_ROWS]]), "dp", -1)
    halo_acts = jnp.concatenate([before, after[:HALO_ROWS]])
    halo_cots = jnp.concatenate([jnp.zeros_like(before), after[HALO_ROWS:]])
    own_rows = inverse_rows(basis_store[0], lambda_store[0])
    adjoint, partial = window(query_acts, cotangent, halo_acts, halo_cots, conv_weight, conv_bias)
    held = jnp.where((owner_map == here)[:, None, None], own_rows[None], 0.0)
    inverse = lax.psum(held, "dp")
    summed = (lax.psum(partial, "dp") * norm_scale).reshape(layers, 5, channels)
    order = {pair: i for i, pair in enumerate(PAIRS)}
    everyone = jnp.stack([
        sum(inverse[:, order[min(j, k), max(j, k)]] * summed[:, k] for k in range(5))
        for j in range(5)
    ], axis=1)
    return adjoint, everyone


def on_device(query_acts, cotangent, conv_weight, conv_bias, owner_map, basis_store, lambda_store,
              train_grads, batch_index):
    rows, channels = query_acts.shape
    layers = conv_weight.shape[0]
    count = lax.axis_size("dp")
    here = lax.axis_index("dp")
    norm_scale = 1.0 / math.sqrt(rows * count)
    lines = channels // (LANES * count)
    examples = train_grads.shape[0]
    final = 1.0 / math.sqrt(5 * layers * channels)
    if lines in (4, 8) and count % 4 == 0 and channels == lines * LANES * count and (
            rows % HALO == 0 and batch_index.shape[0] <= LANES):
        moved, values = fused(query_acts, cotangent, conv_weight, conv_bias, owner_map, basis_store[0],
                                lambda_store[0], train_grads.transpose(0, 2, 1, 3), norm_scale, final)
        adjoint, scores = finish(moved, values, batch_index, rows)
        return (adjoint, scores.reshape(-1))
    else:
        adjoint, everyone = precondition_apart(query_acts, cotangent, conv_weight, conv_bias, owner_map,
                                               basis_store, lambda_store, norm_scale)
        high = everyone.astype(jnp.bfloat16)
        low = (everyone - high.astype(jnp.float32)).astype(jnp.bfloat16)
        both = high.astype(jnp.float32) + low.astype(jnp.float32)
        values = jnp.sum(train_grads.astype(jnp.float32) * both[None], axis=(1, 2, 3)) * final
    local_index = batch_index - here * examples
    chosen = local_index[:, None] == jnp.arange(examples, dtype=jnp.int32)[None, :]
    scores = jnp.sum(jnp.where(chosen, values[None, :], 0.0), axis=1)
    return (adjoint, scores)


def solution(mesh):
    in_specs = (
        P(("groups", "dp"), None),
        P(("groups", "dp"), None),
        P(),
        P(),
        P(),
        P("dp", None, None),
        P("dp", None, None),
        P(("groups", "dp"), None, None, None),
        P(("groups", "dp")),
    )
    out_specs = (P(("groups", "dp"), None), P(("groups", "dp")))
    return jax.shard_map(
        on_device, mesh=mesh, in_specs=in_specs, out_specs=out_specs, check_vma=False
    )
```

```python
import functools
import math

import jax
import jax.numpy as jnp
import numpy as np
from jax import lax
from jax.experimental import pallas as pl
from jax.experimental.pallas import tpu as pltpu
from jax.sharding import PartitionSpec as P

LANES = 128
SUB = 8
TAPS = 4
HALO_ROWS = 16
PAIRS = [(j, k) for j in range(5) for k in range(j, 5)]


def layout_plan(rows, layers):
    reach = (TAPS - 1) * layers
    extended = rows + 2 * reach
    fold = -(-extended // SUB)
    padded = -(-(fold * SUB) // 16) * 16
    return reach, fold, padded


def permutations(rows, layers):
    reach, fold, padded = layout_plan(rows, layers)
    columns = rows + 2 * HALO_ROWS
    into = np.zeros((padded, columns), np.float32)
    back = np.zeros((rows, padded), np.float32)
    for j in range(fold):
        for s in range(SUB):
            token = fold * s + j - reach
            row = SUB * j + s
            if 0 <= token < rows:
                into[row, token] = 1.0
                back[token, row] = 1.0
            elif -reach <= token < 0:
                into[row, rows + HALO_ROWS + token] = 1.0
            elif rows <= token < rows + reach:
                into[row, HALO_ROWS + token] = 1.0
    return jnp.asarray(into, jnp.bfloat16), jnp.asarray(back, jnp.bfloat16)


def rounded(value):
    return value.astype(jnp.bfloat16).astype(jnp.float32)


def window_chunk(lanes, rows, layers, is_first, w_ref, b_ref, x_all, c_all, slope_all, g_ref):
    reach, fold, padded = layout_plan(rows, layers)
    sub = lax.broadcasted_iota(jnp.int32, (SUB, LANES), 0)
    edges = {}

    def own(j, low, high):
        tokens = [fold * s + j - reach for s in range(SUB)]
        inside = tuple(low <= t < high for t in tokens)
        if all(inside):
            return None
        if inside not in edges:
            lead = next(i for i, ok in enumerate(inside) if ok)
            tail = max(i for i, ok in enumerate(inside) if ok)
            edges[inside] = (sub >= lead) & (sub <= tail)
        return edges[inside]

    zero = jnp.zeros((SUB, LANES), jnp.float32)

    def keep(value, mask):
        return value if mask is None else jnp.where(mask, value, zero)

    def row(ref, *at):
        return jnp.broadcast_to(ref[at[:-1] + (pl.ds(at[-1], 1), lanes)], (SUB, LANES))

    live = {}

    def begun(j):
        mask = own(j, 0, 1 << 30)
        if mask is None:
            return None
        key = id(mask)
        if key not in live:
            live[key] = mask | jnp.logical_not(is_first)
        return live[key]

    last = TAPS - 1
    for layer in range(layers):
        taps = [row(w_ref, layer, k) * 0.5 for k in range(TAPS)]
        bias = row(b_ref, layer) * 0.5
        base = layer * (fold + last) * SUB
        for i in range(last):
            wrapped = x_all[pl.ds(base + (fold + i) * SUB, SUB), lanes]
            x_all[pl.ds(base + i * SUB, SUB), lanes] = pltpu.roll(wrapped, 1, 0)
        x = [x_all[pl.ds(base + i * SUB, SUB), lanes] for i in range(fold + last)]
        following = base + (fold + last + last) * SUB
        for j in range(fold):
            half = bias
            for k in range(TAPS):
                half = half + taps[k] * x[last + j - k]
            bent = jnp.tanh(half)
            up = 1.0 + bent
            slope_all[pl.ds((layer * fold + j) * SUB, SUB), lanes] = up * (1.0 + half * (1.0 - bent))
            if layer < layers - 1:
                fresh = keep(rounded(x[last + j] + half * up), begun(j))
                x_all[pl.ds(following + j * SUB, SUB), lanes] = fresh
    for layer in reversed(range(layers)):
        taps = [row(w_ref, layer, k) * 0.5 for k in range(TAPS)]
        base = layer * (fold + last) * SUB
        doubled = [None] * (fold + last)
        sums = [zero] * (TAPS + 1)

        def at(i):
            return x_all[pl.ds(base + i * SUB, SUB), lanes]

        for j in range(fold):
            adjoint = c_all[pl.ds(j * SUB, SUB), lanes]
            slope = slope_all[pl.ds((layer * fold + j) * SUB, SUB), lanes]
            grad = keep(rounded(adjoint * slope), own(j, 0, 1 << 30))
            doubled[j] = grad
            if j < last:
                doubled[fold + j] = pltpu.roll(grad, SUB - 1, 0)
            inner = keep(grad, own(j, -(1 << 30), rows))
            for k in range(TAPS):
                sums[k] = sums[k] + at(last + j - k) * inner
            sums[TAPS] = sums[TAPS] + inner
        for j in range(fold):
            total = c_all[pl.ds(j * SUB, SUB), lanes]
            back = taps[0] * doubled[j]
            for k in range(1, TAPS):
                back = back + taps[k] * doubled[j + k]
            c_all[pl.ds(j * SUB, SUB), lanes] = rounded(total + back)
        for k in range(TAPS + 1):
            g_ref[pl.ds(layer * 5 + k, 1), lanes] = 0.5 * jnp.sum(sums[k], axis=0, keepdims=True)


def window_kernel(rows, layers, x_ref, c_ref, hx_ref, hc_ref, w_ref, b_ref, into_ref, back_ref,
                  out_ref, g_ref, x_all, c_all, slope_all):
    reach, fold, padded = layout_plan(rows, layers)
    width = x_ref.shape[1]
    is_first = lax.axis_index("dp") == 0
    count = fold * SUB
    acts = jnp.concatenate([x_ref[...], hx_ref[...]], axis=0)
    cots = jnp.concatenate([c_ref[...], hc_ref[...]], axis=0)
    x_all[pl.ds((TAPS - 1) * SUB, count), :] = jnp.dot(
        into_ref[...], acts, preferred_element_type=jnp.float32)[:count]
    c_all[...] = jnp.dot(into_ref[...], cots, preferred_element_type=jnp.float32)

    @pl.loop(0, width // LANES)
    def _(chunk):
        lanes = pl.ds(pl.multiple_of(chunk * LANES, LANES), LANES)
        window_chunk(lanes, rows, layers, is_first, w_ref, b_ref, x_all, c_all, slope_all, g_ref)

    out_ref[...] = jnp.dot(
        back_ref[...], c_all[...].astype(jnp.bfloat16), preferred_element_type=jnp.float32
    ).astype(jnp.bfloat16)


def window(acts, cots, halo_acts, halo_cots, weights, bias):
    rows, channels = acts.shape
    layers = weights.shape[0]
    reach, fold, padded = layout_plan(rows, layers)
    width = 512
    into, back = permutations(rows, layers)
    block = lambda *lead: pl.BlockSpec(lead + (width,), lambda i: (0,) * len(lead) + (i,))
    whole = lambda a: pl.BlockSpec(a.shape, lambda i: (0, 0))
    return pl.pallas_call(
        functools.partial(window_kernel, rows, layers),
        grid=(channels // width,),
        out_shape=(
            jax.ShapeDtypeStruct((rows, channels), jnp.bfloat16),
            jax.ShapeDtypeStruct((layers * 5, channels), jnp.float32),
        ),
        in_specs=[
            block(rows), block(rows), block(2 * HALO_ROWS), block(2 * HALO_ROWS),
            block(layers, TAPS), block(layers), whole(into), whole(back),
        ],
        out_specs=(block(rows), block(layers * 5)),
        scratch_shapes=[
            pltpu.VMEM((layers * (fold + TAPS - 1) * SUB, width), jnp.float32),
            pltpu.VMEM((padded, width), jnp.float32),
            pltpu.VMEM((layers * fold * SUB, width), jnp.float32),
        ],
        compiler_params=pltpu.CompilerParams(vmem_limit_bytes=24 << 20),
        cost_estimate=pl.CostEstimate(flops=200_000_000, bytes_accessed=10_000_000, transcendentals=5_000_000),
    )(acts, cots, halo_acts, halo_cots, weights, bias, into, back)


def shifted(value, axis, steps):
    count = lax.axis_size(axis)
    first, final = (max(0, -steps), min(count, count - steps))
    return lax.ppermute(value, axis, [(s, s + steps) for s in range(first, final)])


def inverse_rows(basis, vals):
    channels = basis.shape[-1]
    blocks = basis.reshape(5, 5, channels)
    scale = 1.0 / (vals + 0.1 * jnp.mean(vals))
    return jnp.stack([jnp.sum(blocks[j] * blocks[k] * scale, axis=0) for j, k in PAIRS])


ROWS8 = 8
HALO = 16


def token_permutation(invert):
    row = lax.broadcasted_iota(jnp.int32, (LANES, LANES), 0)
    col = lax.broadcasted_iota(jnp.int32, (LANES, LANES), 1)
    if invert:
        row, col = col, row
    same = ((row >> 3) == (col & 15)) & ((row & 7) == (col >> 4))
    return jnp.where(same, 1.0, 0.0).astype(jnp.bfloat16)


def forward_layer(layer, layers, rows, step, tile, x_all, s_all, w_all, keep):
    taps = [w_all[layer * TAPS + k, tile, :] * 0.5 for k in range(TAPS)]
    bias = w_all[layers * TAPS + layer, tile, :] * 0.5

    def span(first, n, mask=None):
        x = [x_all[layer, first - 3 + i] for i in range(n + 3)]
        for i in range(n):
            half = ((taps[0] * x[i + 3] + taps[1] * x[i + 2]) + (taps[2] * x[i + 1] + taps[3] * x[i])) + bias
            bent = jnp.tanh(half)
            up = 1.0 + bent
            gain = half * up
            s_all[layer, first + i] = up + gain * (1.0 - bent)
            if layer < layers - 1:
                fresh = x[i + 3] + gain
                x_all[layer + 1, first + i] = fresh if mask is None else fresh * mask

    early = 3 * (layers - 1 - layer)
    if early:
        span(HALO - early, early, keep)
    total = rows + 3 * layers
    full, rest = total // step, total % step

    @pl.loop(0, full)
    def _(j):
        span(HALO + j * step, step)

    if rest:
        span(HALO + full * step, rest)


def pairwise(values):
    while len(values) > 1:
        values = [values[i] + values[i + 1] if i + 1 < len(values) else values[i]
                  for i in range(0, len(values), 2)]
    return values[0]


def backward_layer(layer, layers, rows, step, tile, x_all, s_all, a_all, w_all, g_all):
    taps = [w_all[layer * TAPS + k, tile, :] * 0.5 for k in range(TAPS)]

    def grads(first, n):
        return [a_all[first + i] * s_all[layer, HALO + first + i] for i in range(n)]

    def back(first, dv, n):
        for i in range(n):
            a_all[first + i] = a_all[first + i] + (
                (taps[0] * dv[i] + taps[1] * dv[i + 1]) + (taps[2] * dv[i + 2] + taps[3] * dv[i + 3]))

    def sums(first, dv, n):
        x = [x_all[layer, HALO + first - 3 + i] for i in range(n + 3)]
        terms = [pairwise([x[i + 3 - k] * dv[i] for i in range(n)]) for k in range(TAPS)]
        return terms + [pairwise(dv[:n])]

    def body(j, carry):
        first = j * step
        dv = list(carry[:3]) + grads(first + 3, step)
        part = sums(first, dv, step)
        back(first, dv, step)
        return tuple(dv[step:step + 3]) + tuple(a + b for a, b in zip(carry[3:], part))

    zero = jnp.zeros((ROWS8, LANES), jnp.float32)
    carry = lax.fori_loop(0, rows // step, body, tuple(grads(0, 3)) + (zero,) * (TAPS + 1))
    for k in range(TAPS + 1):
        g_all[layer * 5 + k] = 0.5 * carry[3 + k]
    extra = 3 * layer
    if extra:
        dv = list(carry[:3]) + grads(rows + 3, extra)
        back(rows, dv, extra)


def fused_kernel(count, layers, rows, channels, scale, final, o_hbm, x_hbm, c_hbm, w_hbm, b_hbm, q_hbm, l_hbm, t_hbm,
                 out_hbm, p_ref, xh, ch, wv, bv, qv, lv, w_all, x_all, s_all, a_all, g_all, ov, ot,
                 ms, got_m, gs, got_g, part, full_p, tv, sacc, owner_ref,
                 load, store, send_h, recv_h, send_m, recv_m, send_g, recv_g, send_p, recv_p):
    here = lax.axis_index("dp")
    width = ROWS8 * LANES
    groups = channels // width
    share = channels // count
    lines = share // LANES
    per = ROWS8 // lines

    def remote(source, target_ref, sent, got, device):
        return pltpu.make_async_remote_copy(
            src_ref=source, dst_ref=target_ref, send_sem=sent, recv_sem=got,
            device_id={"dp": device}, device_id_type=pl.DeviceIdType.MESH)

    locals_ = [
        pltpu.make_async_copy(q_hbm, qv, load.at[0]),
        pltpu.make_async_copy(l_hbm, lv, load.at[1]),
        pltpu.make_async_copy(w_hbm, wv, load.at[2]),
        pltpu.make_async_copy(b_hbm, bv, load.at[3]),
        pltpu.make_async_copy(x_hbm, xh.at[pl.ds(HALO, rows), :], load.at[4]),
        pltpu.make_async_copy(c_hbm, ch.at[pl.ds(0, rows), :], load.at[5]),
        pltpu.make_async_copy(o_hbm, owner_ref, load.at[6]),
        pltpu.make_async_copy(t_hbm, tv, load.at[7]),
    ]
    for copy in locals_:
        copy.start()
    barrier = pltpu.get_barrier_semaphore()

    @pl.loop(1, count)
    def _(step):
        pl.semaphore_signal(barrier, inc=1, device_id={"dp": lax.rem(here + step, count)},
                            device_id_type=pl.DeviceIdType.MESH)

    pl.semaphore_wait(barrier, count - 1)

    def lanes_of(group):
        return pl.ds(pl.multiple_of(group * width, width), width)

    def group_at(device, i):
        return lax.rem(lax.div(device, per) + 1 + i, groups)

    def halo(kind, group, device):
        lanes = lanes_of(group)
        if kind == 0:
            source, target = x_hbm.at[pl.ds(rows - HALO, HALO), lanes], xh.at[pl.ds(0, HALO), lanes]
        elif kind == 1:
            source, target = x_hbm.at[pl.ds(0, HALO), lanes], xh.at[pl.ds(rows + HALO, HALO), lanes]
        else:
            source, target = c_hbm.at[pl.ds(0, HALO), lanes], ch.at[pl.ds(rows, HALO), lanes]
        return remote(source, target, send_h.at[kind, group], recv_h.at[kind, group], device)

    def send_halos(turn):
        @pl.when(here < count - 1)
        def _():
            halo(0, group_at(here + 1, turn), here + 1).start()

        @pl.when(here > 0)
        def _():
            group = group_at(here - 1, turn)
            halo(1, group, here - 1).start()
            halo(2, group, here - 1).start()

    ahead = 2
    for turn in range(ahead):
        send_halos(turn)

    @pl.when(here == 0)
    def _():
        xh[pl.ds(0, HALO), :] = jnp.zeros((HALO, channels), jnp.bfloat16)

    @pl.when(here == count - 1)
    def _():
        xh[pl.ds(rows + HALO, HALO), :] = jnp.zeros((HALO, channels), jnp.bfloat16)
        ch[pl.ds(rows, HALO), :] = jnp.zeros((HALO, channels), jnp.bfloat16)

    locals_[0].wait()
    locals_[1].wait()
    damping = 0.1 * jnp.mean(lv[...])

    @pl.loop(0, groups)
    def _(o):
        tile = pl.ds(pl.multiple_of(o * ROWS8, ROWS8), ROWS8)
        inverse = [1.0 / (lv[i, tile, :] + damping) for i in range(5)]
        basis = [[qv[j * 5 + i, tile, :] for i in range(5)] for j in range(5)]
        for at, (j, k) in enumerate(PAIRS):
            value = basis[j][0] * basis[k][0] * inverse[0]
            for i in range(1, 5):
                value = value + basis[j][i] * basis[k][i] * inverse[i]
            for h in range(per):
                ms[o * per + h, at] = value[h * lines:(h + 1) * lines].astype(jnp.bfloat16)

    def send_rows(step):
        target = lax.rem(here + step, count)
        return remote(ms.at[target], got_m.at[step], send_m.at[step], recv_m.at[step], target)

    got_m[0] = ms[here]
    locals_[2].wait()
    locals_[3].wait()

    @pl.loop(0, channels // LANES)
    def _(g):
        lanes = pl.ds(pl.multiple_of(g * LANES, LANES), LANES)
        for layer in range(layers):
            for k in range(TAPS):
                w_all[layer * TAPS + k, pl.ds(g, 1), :] = wv[layer, pl.ds(k, 1), lanes]
            w_all[layers * TAPS + layer, pl.ds(g, 1), :] = bv[pl.ds(layer, 1), lanes]

    into, back = token_permutation(False), token_permutation(True)
    keep = jnp.where(here > 0, 1.0, 0.0) * jnp.ones((ROWS8, LANES), jnp.float32)
    locals_[4].wait()
    locals_[5].wait()

    def gather_block(ref, at, base):
        return jnp.concatenate(
            [ref[pl.ds(at, HALO), pl.ds(pl.multiple_of(base + g * LANES, LANES), LANES)] for g in range(ROWS8)],
            axis=0)

    def give(group, h):
        owner = group * per + h
        return remote(gs.at[owner], got_g.at[here], send_g.at[owner], recv_g.at[here], owner)

    def written(group):
        return pltpu.make_async_copy(ot.at[:, lanes_of(group)], out_hbm.at[:, lanes_of(group)], store.at[group])

    @pl.loop(0, groups)
    def _(turn):
        group = group_at(here, turn)
        base = group * width
        tile = pl.ds(pl.multiple_of(group * ROWS8, ROWS8), ROWS8)

        @pl.when(turn < groups - ahead)
        def _():
            send_halos(turn + ahead)

        @pl.when(here > 0)
        def _():
            halo(0, group, here - 1).wait_recv()

        @pl.when(here < count - 1)
        def _():
            halo(1, group, here + 1).wait_recv()
            halo(2, group, here + 1).wait_recv()

        def arrange(source, target, blocks):
            wide = jnp.concatenate([gather_block(source, b * HALO, base) for b in range(blocks)], axis=1)
            moved = jnp.dot(into, wide, preferred_element_type=jnp.float32)
            for b in range(blocks):
                target[pl.ds(b * HALO, HALO)] = moved[:, b * LANES:(b + 1) * LANES].reshape(HALO, ROWS8, LANES)

        arrange(xh, x_all.at[0], rows // HALO + 2)
        arrange(ch, a_all, rows // HALO + 1)

        for layer in range(layers):
            forward_layer(layer, layers, rows, (rows + 3 * layers) // 2, tile, x_all, s_all, w_all, keep)
        for layer in reversed(range(layers)):
            backward_layer(layer, layers, rows, 16, tile, x_all, s_all, a_all, w_all, g_all)

        for h in range(per):
            for term in range(layers * 5):
                gs[group * per + h, term] = g_all[term, h * lines:(h + 1) * lines].astype(jnp.bfloat16)

        for h in range(per):
            @pl.when(group * per + h != here)
            def _():
                give(group, h).start()

        ov[group] = a_all[pl.ds(0, rows)].reshape(rows * ROWS8, LANES).astype(jnp.bfloat16)
        @pl.when(turn == 0)
        def _():
            @pl.loop(1, count)
            def _(step):
                send_rows(step).start()

    @pl.loop(1, count)
    def _(step):
        send_rows(step).wait()

    @pl.loop(1, count)
    def _(step):
        source = lax.rem(here + step, count)
        remote(gs.at[source], got_g.at[source], send_g.at[source], recv_g.at[source], source).wait()

    locals_[6].wait()
    total = gs[here].astype(jnp.float32)
    for step in range(1, count):
        total = total + got_g[lax.rem(here + step, count)].astype(jnp.float32)
    total = total * scale
    order = {pair: i for i, pair in enumerate(PAIRS)}
    for layer in range(layers):
        slot = lax.rem(here - owner_ref[layer] + count, count)
        inverse = got_m[slot].astype(jnp.float32)
        for j in range(5):
            value = None
            for k in range(5):
                term = inverse[order[min(j, k), max(j, k)]] * total[layer * 5 + k]
                value = term if value is None else value + term
            for r in range(lines):
                part[j, pl.ds(layer, 1), r * LANES:(r + 1) * LANES] = value[r:r + 1]

    core, side, depth = lax.rem(here, 2), lax.rem(lax.div(here, 2), 2), count // 4
    mate = here + 1 - 2 * core
    across = here + 2 - 4 * side

    def along(device, i):
        return lax.rem(device + 4 * i, count)

    def span_of(owner):
        return pl.ds(pl.multiple_of(owner * share, share), share)

    def pass_on(owner, target, slot):
        lanes = span_of(owner)
        return remote(full_p.at[:, :, lanes], full_p.at[:, :, lanes], send_p.at[slot], recv_p.at[owner], target)

    def score(owner):
        lanes = span_of(owner)
        both = []
        for j in range(5):
            value = full_p[j, :, lanes]
            high = value.astype(jnp.bfloat16).astype(jnp.float32)
            both.append(high + (value - high).astype(jnp.bfloat16).astype(jnp.float32))
        for e in range(tv.shape[0]):
            value = tv[e, 0, :, lanes].astype(jnp.float32) * both[0]
            for j in range(1, 5):
                value = value + tv[e, j, :, lanes].astype(jnp.float32) * both[j]
            sacc[e] = sacc[e] + value

    full_p[:, :, span_of(here)] = part[...]
    sends = []

    def send(owner, target):
        copy = pass_on(owner, target, len(sends))
        copy.start()
        sends.append(copy)

    def await_part(owner):
        pass_on(owner, mate, 0).wait_recv()

    for i in range(1, depth):
        send(here, along(here, i))
    send(here, across)
    send(here, mate)
    @pl.loop(0, groups)
    def _(group):
        blocks = rows // HALO
        wide = jnp.concatenate([ov[group, pl.ds(b * LANES, LANES), :] for b in range(blocks)], axis=1)
        moved = jnp.dot(back, wide, preferred_element_type=jnp.float32).astype(jnp.bfloat16)
        for b in range(blocks):
            for g in range(ROWS8):
                lanes = pl.ds(pl.multiple_of(group * width + g * LANES, LANES), LANES)
                ot[pl.ds(b * HALO, HALO), lanes] = moved[g * HALO:(g + 1) * HALO, b * LANES:(b + 1) * LANES]
        written(group).start()

    sacc[...] = jnp.zeros_like(sacc)
    locals_[7].wait()
    score(here)
    for i in range(1, depth):
        await_part(along(here, i))
        send(along(here, i), across)
        send(along(here, i), mate)
    await_part(across)
    send(across, mate)
    for i in range(1, depth):
        score(along(here, i))
    for i in range(1, depth):
        await_part(along(across, i))
        send(along(across, i), mate)
    for i in range(depth):
        score(along(across, i))
    for owner in (mate, mate + 2 - 4 * side):
        for i in range(depth):
            await_part(along(owner, i))
            score(along(owner, i))

    for e in range(tv.shape[0]):
        rowed = jnp.sum(jnp.sum(sacc[e], axis=0, keepdims=True), axis=1, keepdims=True)
        p_ref[pl.ds(e, 1), :] = jnp.broadcast_to(rowed * final, (1, LANES))

    @pl.loop(0, groups)
    def _(i):
        written(i).wait()

        @pl.when(here < count - 1)
        def _():
            halo(0, i, here + 1).wait_send()

        @pl.when(here > 0)
        def _():
            halo(1, i, here - 1).wait_send()
            halo(2, i, here - 1).wait_send()

    for copy in sends:
        copy.wait_send()


def fused(acts, cots, weights, bias, owner_map, basis, vals, train, scale, final):
    rows, channels = acts.shape
    layers = weights.shape[0]
    count = lax.axis_size("dp")
    share = channels // count
    lines = share // LANES
    groups = channels // (ROWS8 * LANES)
    held = rows + 2 * HALO
    vmem = pl.BlockSpec(memory_space=pltpu.VMEM)
    anywhere = pl.BlockSpec(memory_space=pltpu.HBM)
    dma = pltpu.SemaphoreType.DMA
    f32, b16 = jnp.float32, jnp.bfloat16
    tall = channels // LANES
    return pl.pallas_call(
        functools.partial(fused_kernel, count, layers, rows, channels, scale, final),
        out_shape=(
            jax.ShapeDtypeStruct((rows, channels), b16),
            jax.ShapeDtypeStruct((train.shape[0], LANES), f32),
        ),
        in_specs=[anywhere] * 8,
        out_specs=(anywhere, vmem),
        scratch_shapes=[
            pltpu.VMEM((held, channels), b16),
            pltpu.VMEM((rows + HALO, channels), b16),
            pltpu.VMEM(weights.shape, f32),
            pltpu.VMEM(bias.shape, f32),
            pltpu.VMEM((25, tall, LANES), f32),
            pltpu.VMEM((5, tall, LANES), f32),
            pltpu.VMEM((layers * 5, tall, LANES), f32),
            pltpu.VMEM((layers, held, ROWS8, LANES), f32),
            pltpu.VMEM((layers, held, ROWS8, LANES), f32),
            pltpu.VMEM((rows + HALO, ROWS8, LANES), f32),
            pltpu.VMEM((layers * 5, ROWS8, LANES), f32),
            pltpu.VMEM((groups, rows * ROWS8, LANES), b16),
            pltpu.VMEM((rows, channels), b16),
            pltpu.VMEM((count, len(PAIRS), lines, LANES), b16),
            pltpu.VMEM((count, len(PAIRS), lines, LANES), b16),
            pltpu.VMEM((count, layers * 5, lines, LANES), b16),
            pltpu.VMEM((count, layers * 5, lines, LANES), b16),
            pltpu.VMEM((5, layers, share), f32),
            pltpu.VMEM((5, layers, channels), f32),
            pltpu.VMEM(train.shape, b16),
            pltpu.VMEM((train.shape[0], layers, share), f32),
            pltpu.SMEM(owner_map.shape, owner_map.dtype),
            dma((8,)), dma((groups,)),
            dma((3, groups)), dma((3, groups)),
            dma((count,)), dma((count,)), dma((count,)), dma((count,)), dma((count,)), dma((count,)),
        ],
        compiler_params=pltpu.CompilerParams(
            collective_id=0, has_side_effects=True, vmem_limit_bytes=63 << 20),
    )(owner_map, acts, cots, weights, bias, basis.reshape(25, tall, LANES), vals.reshape(5, tall, LANES), train)


def finish_kernel(pieces, a_hbm, v_hbm, i_hbm, out_hbm, s_hbm, held, v_ref, i_ref, s_ref, load, store, small):
    width = a_hbm.shape[0] // pieces
    slabs = [pl.ds(i * width, width) for i in range(pieces)]
    reads = [pltpu.make_async_copy(a_hbm.at[slab, :], held.at[slab, :], load.at[i]) for i, slab in enumerate(slabs)]
    writes = [pltpu.make_async_copy(held.at[slab, :], out_hbm.at[slab, :], store.at[i])
              for i, slab in enumerate(slabs)]
    loads = [pltpu.make_async_copy(v_hbm, v_ref, small.at[0]), pltpu.make_async_copy(i_hbm, i_ref, small.at[1])]
    for copy in reads + loads:
        copy.start()
    for copy, onward in zip(reads, writes):
        copy.wait()
        onward.start()
    for copy in loads:
        copy.wait()
    examples = v_ref.shape[0]
    picks = i_ref.shape[1]
    local = i_ref[...] - lax.axis_index("dp") * examples
    chosen = jnp.broadcast_to(local, (examples, picks)) == lax.broadcasted_iota(jnp.int32, (examples, picks), 0)
    s_ref[...] = jnp.sum(jnp.where(chosen, v_ref[:, :picks], 0.0), axis=0, keepdims=True)
    picked = pltpu.make_async_copy(s_ref, s_hbm, small.at[2])
    picked.start()
    for copy in writes:
        copy.wait()
    picked.wait()


def finish(moved, values, batch_index):
    picks = batch_index.shape[0]
    pieces = 8
    anywhere = pl.BlockSpec(memory_space=pltpu.HBM)
    return pl.pallas_call(
        functools.partial(finish_kernel, pieces),
        out_shape=(
            jax.ShapeDtypeStruct(moved.shape, moved.dtype),
            jax.ShapeDtypeStruct((1, picks), jnp.float32),
        ),
        in_specs=[anywhere] * 3,
        out_specs=(anywhere, anywhere),
        scratch_shapes=[
            pltpu.VMEM(moved.shape, moved.dtype),
            pltpu.VMEM(values.shape, values.dtype),
            pltpu.VMEM((1, picks), batch_index.dtype),
            pltpu.VMEM((1, picks), jnp.float32),
            pltpu.SemaphoreType.DMA((pieces,)),
            pltpu.SemaphoreType.DMA((pieces,)),
            pltpu.SemaphoreType.DMA((3,)),
        ],
        compiler_params=pltpu.CompilerParams(vmem_limit_bytes=63 << 20),
    )(moved, values, batch_index.reshape(1, picks))


def precondition_apart(query_acts, cotangent, conv_weight, conv_bias, owner_map, basis_store, lambda_store,
                       norm_scale):
    rows, channels = query_acts.shape
    layers = conv_weight.shape[0]
    here = lax.axis_index("dp")
    before = shifted(query_acts[rows - HALO_ROWS:], "dp", 1)
    after = shifted(jnp.concatenate([query_acts[:HALO_ROWS], cotangent[:HALO_ROWS]]), "dp", -1)
    halo_acts = jnp.concatenate([before, after[:HALO_ROWS]])
    halo_cots = jnp.concatenate([jnp.zeros_like(before), after[HALO_ROWS:]])
    own_rows = inverse_rows(basis_store[0], lambda_store[0])
    adjoint, partial = window(query_acts, cotangent, halo_acts, halo_cots, conv_weight, conv_bias)
    held = jnp.where((owner_map == here)[:, None, None], own_rows[None], 0.0)
    inverse = lax.psum(held, "dp")
    summed = (lax.psum(partial, "dp") * norm_scale).reshape(layers, 5, channels)
    order = {pair: i for i, pair in enumerate(PAIRS)}
    everyone = jnp.stack([
        sum(inverse[:, order[min(j, k), max(j, k)]] * summed[:, k] for k in range(5))
        for j in range(5)
    ], axis=1)
    return adjoint, everyone


def on_device(query_acts, cotangent, conv_weight, conv_bias, owner_map, basis_store, lambda_store,
              train_grads, batch_index):
    rows, channels = query_acts.shape
    layers = conv_weight.shape[0]
    count = lax.axis_size("dp")
    here = lax.axis_index("dp")
    norm_scale = 1.0 / math.sqrt(rows * count)
    lines = channels // (LANES * count)
    examples = train_grads.shape[0]
    final = 1.0 / math.sqrt(5 * layers * channels)
    if lines in (4, 8) and count % 4 == 0 and channels == lines * LANES * count and (
            rows % HALO == 0 and batch_index.shape[0] <= LANES):
        moved, values = fused(query_acts, cotangent, conv_weight, conv_bias, owner_map, basis_store[0],
                                lambda_store[0], train_grads.transpose(0, 2, 1, 3), norm_scale, final)
        adjoint, scores = finish(moved, values, batch_index)
        return (adjoint, scores.reshape(-1))
    else:
        adjoint, everyone = precondition_apart(query_acts, cotangent, conv_weight, conv_bias, owner_map,
                                               basis_store, lambda_store, norm_scale)
        high = everyone.astype(jnp.bfloat16)
        low = (everyone - high.astype(jnp.float32)).astype(jnp.bfloat16)
        both = high.astype(jnp.float32) + low.astype(jnp.float32)
        values = jnp.sum(train_grads.astype(jnp.float32) * both[None], axis=(1, 2, 3)) * final
    local_index = batch_index - here * examples
    chosen = local_index[:, None] == jnp.arange(examples, dtype=jnp.int32)[None, :]
    scores = jnp.sum(jnp.where(chosen, values[None, :], 0.0), axis=1)
    return (adjoint, scores)


def solution(mesh):
    in_specs = (
        P(("groups", "dp"), None),
        P(("groups", "dp"), None),
        P(),
        P(),
        P(),
        P("dp", None, None),
        P("dp", None, None),
        P(("groups", "dp"), None, None, None),
        P(("groups", "dp")),
    )
    out_specs = (P(("groups", "dp"), None), P(("groups", "dp")))
    return jax.shard_map(
        on_device, mesh=mesh, in_specs=in_specs, out_specs=out_specs, check_vma=False
    )
```

```python
import functools
import math

import jax
import jax.numpy as jnp
import numpy as np
from jax import lax
from jax.experimental import pallas as pl
from jax.experimental.pallas import tpu as pltpu
from jax.sharding import PartitionSpec as P

LANES = 128
SUB = 8
TAPS = 4
HALO_ROWS = 16
PAIRS = [(j, k) for j in range(5) for k in range(j, 5)]


def layout_plan(rows, layers):
    reach = (TAPS - 1) * layers
    extended = rows + 2 * reach
    fold = -(-extended // SUB)
    padded = -(-(fold * SUB) // 16) * 16
    return reach, fold, padded


def permutations(rows, layers):
    reach, fold, padded = layout_plan(rows, layers)
    columns = rows + 2 * HALO_ROWS
    into = np.zeros((padded, columns), np.float32)
    back = np.zeros((rows, padded), np.float32)
    for j in range(fold):
        for s in range(SUB):
            token = fold * s + j - reach
            row = SUB * j + s
            if 0 <= token < rows:
                into[row, token] = 1.0
                back[token, row] = 1.0
            elif -reach <= token < 0:
                into[row, rows + HALO_ROWS + token] = 1.0
            elif rows <= token < rows + reach:
                into[row, HALO_ROWS + token] = 1.0
    return jnp.asarray(into, jnp.bfloat16), jnp.asarray(back, jnp.bfloat16)


def rounded(value):
    return value.astype(jnp.bfloat16).astype(jnp.float32)


def window_chunk(lanes, rows, layers, is_first, w_ref, b_ref, x_all, c_all, slope_all, g_ref):
    reach, fold, padded = layout_plan(rows, layers)
    sub = lax.broadcasted_iota(jnp.int32, (SUB, LANES), 0)
    edges = {}

    def own(j, low, high):
        tokens = [fold * s + j - reach for s in range(SUB)]
        inside = tuple(low <= t < high for t in tokens)
        if all(inside):
            return None
        if inside not in edges:
            lead = next(i for i, ok in enumerate(inside) if ok)
            tail = max(i for i, ok in enumerate(inside) if ok)
            edges[inside] = (sub >= lead) & (sub <= tail)
        return edges[inside]

    zero = jnp.zeros((SUB, LANES), jnp.float32)

    def keep(value, mask):
        return value if mask is None else jnp.where(mask, value, zero)

    def row(ref, *at):
        return jnp.broadcast_to(ref[at[:-1] + (pl.ds(at[-1], 1), lanes)], (SUB, LANES))

    live = {}

    def begun(j):
        mask = own(j, 0, 1 << 30)
        if mask is None:
            return None
        key = id(mask)
        if key not in live:
            live[key] = mask | jnp.logical_not(is_first)
        return live[key]

    last = TAPS - 1
    for layer in range(layers):
        taps = [row(w_ref, layer, k) * 0.5 for k in range(TAPS)]
        bias = row(b_ref, layer) * 0.5
        base = layer * (fold + last) * SUB
        for i in range(last):
            wrapped = x_all[pl.ds(base + (fold + i) * SUB, SUB), lanes]
            x_all[pl.ds(base + i * SUB, SUB), lanes] = pltpu.roll(wrapped, 1, 0)
        x = [x_all[pl.ds(base + i * SUB, SUB), lanes] for i in range(fold + last)]
        following = base + (fold + last + last) * SUB
        for j in range(fold):
            half = bias
            for k in range(TAPS):
                half = half + taps[k] * x[last + j - k]
            bent = jnp.tanh(half)
            up = 1.0 + bent
            slope_all[pl.ds((layer * fold + j) * SUB, SUB), lanes] = up * (1.0 + half * (1.0 - bent))
            if layer < layers - 1:
                fresh = keep(rounded(x[last + j] + half * up), begun(j))
                x_all[pl.ds(following + j * SUB, SUB), lanes] = fresh
    for layer in reversed(range(layers)):
        taps = [row(w_ref, layer, k) * 0.5 for k in range(TAPS)]
        base = layer * (fold + last) * SUB
        doubled = [None] * (fold + last)
        sums = [zero] * (TAPS + 1)

        def at(i):
            return x_all[pl.ds(base + i * SUB, SUB), lanes]

        for j in range(fold):
            adjoint = c_all[pl.ds(j * SUB, SUB), lanes]
            slope = slope_all[pl.ds((layer * fold + j) * SUB, SUB), lanes]
            grad = keep(rounded(adjoint * slope), own(j, 0, 1 << 30))
            doubled[j] = grad
            if j < last:
                doubled[fold + j] = pltpu.roll(grad, SUB - 1, 0)
            inner = keep(grad, own(j, -(1 << 30), rows))
            for k in range(TAPS):
                sums[k] = sums[k] + at(last + j - k) * inner
            sums[TAPS] = sums[TAPS] + inner
        for j in range(fold):
            total = c_all[pl.ds(j * SUB, SUB), lanes]
            back = taps[0] * doubled[j]
            for k in range(1, TAPS):
                back = back + taps[k] * doubled[j + k]
            c_all[pl.ds(j * SUB, SUB), lanes] = rounded(total + back)
        for k in range(TAPS + 1):
            g_ref[pl.ds(layer * 5 + k, 1), lanes] = 0.5 * jnp.sum(sums[k], axis=0, keepdims=True)


def window_kernel(rows, layers, x_ref, c_ref, hx_ref, hc_ref, w_ref, b_ref, into_ref, back_ref,
                  out_ref, g_ref, x_all, c_all, slope_all):
    reach, fold, padded = layout_plan(rows, layers)
    width = x_ref.shape[1]
    is_first = lax.axis_index("dp") == 0
    count = fold * SUB
    acts = jnp.concatenate([x_ref[...], hx_ref[...]], axis=0)
    cots = jnp.concatenate([c_ref[...], hc_ref[...]], axis=0)
    x_all[pl.ds((TAPS - 1) * SUB, count), :] = jnp.dot(
        into_ref[...], acts, preferred_element_type=jnp.float32)[:count]
    c_all[...] = jnp.dot(into_ref[...], cots, preferred_element_type=jnp.float32)

    @pl.loop(0, width // LANES)
    def _(chunk):
        lanes = pl.ds(pl.multiple_of(chunk * LANES, LANES), LANES)
        window_chunk(lanes, rows, layers, is_first, w_ref, b_ref, x_all, c_all, slope_all, g_ref)

    out_ref[...] = jnp.dot(
        back_ref[...], c_all[...].astype(jnp.bfloat16), preferred_element_type=jnp.float32
    ).astype(jnp.bfloat16)


def window(acts, cots, halo_acts, halo_cots, weights, bias):
    rows, channels = acts.shape
    layers = weights.shape[0]
    reach, fold, padded = layout_plan(rows, layers)
    width = 512
    into, back = permutations(rows, layers)
    block = lambda *lead: pl.BlockSpec(lead + (width,), lambda i: (0,) * len(lead) + (i,))
    whole = lambda a: pl.BlockSpec(a.shape, lambda i: (0, 0))
    return pl.pallas_call(
        functools.partial(window_kernel, rows, layers),
        grid=(channels // width,),
        out_shape=(
            jax.ShapeDtypeStruct((rows, channels), jnp.bfloat16),
            jax.ShapeDtypeStruct((layers * 5, channels), jnp.float32),
        ),
        in_specs=[
            block(rows), block(rows), block(2 * HALO_ROWS), block(2 * HALO_ROWS),
            block(layers, TAPS), block(layers), whole(into), whole(back),
        ],
        out_specs=(block(rows), block(layers * 5)),
        scratch_shapes=[
            pltpu.VMEM((layers * (fold + TAPS - 1) * SUB, width), jnp.float32),
            pltpu.VMEM((padded, width), jnp.float32),
            pltpu.VMEM((layers * fold * SUB, width), jnp.float32),
        ],
        compiler_params=pltpu.CompilerParams(vmem_limit_bytes=24 << 20),
        cost_estimate=pl.CostEstimate(flops=200_000_000, bytes_accessed=10_000_000, transcendentals=5_000_000),
    )(acts, cots, halo_acts, halo_cots, weights, bias, into, back)


def shifted(value, axis, steps):
    count = lax.axis_size(axis)
    first, final = (max(0, -steps), min(count, count - steps))
    return lax.ppermute(value, axis, [(s, s + steps) for s in range(first, final)])


def inverse_rows(basis, vals):
    channels = basis.shape[-1]
    blocks = basis.reshape(5, 5, channels)
    scale = 1.0 / (vals + 0.1 * jnp.mean(vals))
    return jnp.stack([jnp.sum(blocks[j] * blocks[k] * scale, axis=0) for j, k in PAIRS])


ROWS8 = 8
HALO = 16


def token_permutation(invert):
    row = lax.broadcasted_iota(jnp.int32, (LANES, LANES), 0)
    col = lax.broadcasted_iota(jnp.int32, (LANES, LANES), 1)
    if invert:
        row, col = col, row
    same = ((row >> 3) == (col & 15)) & ((row & 7) == (col >> 4))
    return jnp.where(same, 1.0, 0.0).astype(jnp.bfloat16)


def forward_layer(layer, layers, rows, step, tile, x_all, s_all, w_all, keep):
    taps = [w_all[layer * TAPS + k, tile, :] * 0.5 for k in range(TAPS)]
    bias = w_all[layers * TAPS + layer, tile, :] * 0.5

    def span(first, n, mask=None):
        x = [x_all[layer, first - 3 + i] for i in range(n + 3)]
        for i in range(n):
            half = ((taps[0] * x[i + 3] + taps[1] * x[i + 2]) + (taps[2] * x[i + 1] + taps[3] * x[i])) + bias
            bent = jnp.tanh(half)
            up = 1.0 + bent
            gain = half * up
            s_all[layer, first + i] = up + gain * (1.0 - bent)
            if layer < layers - 1:
                fresh = x[i + 3] + gain
                x_all[layer + 1, first + i] = fresh if mask is None else fresh * mask

    early = 3 * (layers - 1 - layer)
    if early:
        span(HALO - early, early, keep)
    total = rows + 3 * layers
    full, rest = total // step, total % step

    @pl.loop(0, full)
    def _(j):
        span(HALO + j * step, step)

    if rest:
        span(HALO + full * step, rest)


def pairwise(values):
    while len(values) > 1:
        values = [values[i] + values[i + 1] if i + 1 < len(values) else values[i]
                  for i in range(0, len(values), 2)]
    return values[0]


def backward_layer(layer, layers, rows, step, tile, x_all, s_all, a_all, w_all, g_all, dv_all):
    taps = [w_all[layer * TAPS + k, tile, :] * 0.5 for k in range(TAPS)]

    def grads(first, n):
        return [a_all[first + i] * s_all[layer, HALO + first + i] for i in range(n)]

    def back(first, dv, n):
        for i in range(n):
            a_all[first + i] = a_all[first + i] + (
                (taps[0] * dv[i] + taps[1] * dv[i + 1]) + (taps[2] * dv[i + 2] + taps[3] * dv[i + 3]))

    def sums(first, dv, n):
        x = [x_all[layer, HALO + first - 3 + i] for i in range(n + 3)]
        terms = [pairwise([x[i + 3 - k] * dv[i] for i in range(n)]) for k in range(TAPS)]
        return terms + [pairwise(dv[:n])]

    def body(j, carry):
        first = j * step
        dv = list(carry[:3]) + grads(first + 3, step)
        part = sums(first, dv, step)
        if layer:
            back(first, dv, step)
        else:
            keep_grads(first + 3, dv[3:])
        return tuple(dv[step:step + 3]) + tuple(a + b for a, b in zip(carry[3:], part))

    def keep_grads(first, dv):
        for i, value in enumerate(dv):
            dv_all[first + i] = value

    zero = jnp.zeros((ROWS8, LANES), jnp.float32)
    early = grads(0, 3)
    if not layer:
        keep_grads(0, early)
    carry = lax.fori_loop(0, rows // step, body, tuple(early) + (zero,) * (TAPS + 1))
    for k in range(TAPS + 1):
        g_all[layer * 5 + k] = 0.5 * carry[3 + k]
    extra = 3 * layer
    if extra:
        dv = list(carry[:3]) + grads(rows + 3, extra)
        back(rows, dv, extra)


def fused_kernel(count, layers, rows, channels, scale, final, o_hbm, x_hbm, c_hbm, w_hbm, b_hbm, q_hbm, l_hbm, t_hbm,
                 out_hbm, p_ref, xh, ch, wv, bv, qv, lv, w_all, x_all, s_all, a_all, g_all, dv_all, ot,
                 ms, got_m, gs, gm, fs, got_g, part, full_p, tv, sacc, owner_ref,
                 load, store, send_h, recv_h, send_m, recv_m, send_x, recv_x, send_g, recv_g, send_p, recv_p):
    here = lax.axis_index("dp")
    width = ROWS8 * LANES
    groups = channels // width
    share = channels // count
    lines = share // LANES
    per = ROWS8 // lines

    def remote(source, target_ref, sent, got, device):
        return pltpu.make_async_remote_copy(
            src_ref=source, dst_ref=target_ref, send_sem=sent, recv_sem=got,
            device_id={"dp": device}, device_id_type=pl.DeviceIdType.MESH)

    locals_ = [
        pltpu.make_async_copy(q_hbm, qv, load.at[0]),
        pltpu.make_async_copy(l_hbm, lv, load.at[1]),
        pltpu.make_async_copy(w_hbm, wv, load.at[2]),
        pltpu.make_async_copy(b_hbm, bv, load.at[3]),
        pltpu.make_async_copy(x_hbm, xh.at[pl.ds(HALO, rows), :], load.at[4]),
        pltpu.make_async_copy(c_hbm, ch.at[pl.ds(0, rows), :], load.at[5]),
        pltpu.make_async_copy(o_hbm, owner_ref, load.at[6]),
        pltpu.make_async_copy(t_hbm, tv, load.at[7]),
    ]
    for copy in locals_:
        copy.start()
    barrier = pltpu.get_barrier_semaphore()

    @pl.loop(1, count)
    def _(step):
        pl.semaphore_signal(barrier, inc=1, device_id={"dp": lax.rem(here + step, count)},
                            device_id_type=pl.DeviceIdType.MESH)

    pl.semaphore_wait(barrier, count - 1)

    def lanes_of(group):
        return pl.ds(pl.multiple_of(group * width, width), width)

    def group_at(device, i):
        return lax.rem(lax.div(device, per) + 1 + i, groups)

    def halo(kind, group, device):
        lanes = lanes_of(group)
        if kind == 0:
            source, target = x_hbm.at[pl.ds(rows - HALO, HALO), lanes], xh.at[pl.ds(0, HALO), lanes]
        elif kind == 1:
            source, target = x_hbm.at[pl.ds(0, HALO), lanes], xh.at[pl.ds(rows + HALO, HALO), lanes]
        else:
            source, target = c_hbm.at[pl.ds(0, HALO), lanes], ch.at[pl.ds(rows, HALO), lanes]
        return remote(source, target, send_h.at[kind, group], recv_h.at[kind, group], device)

    def send_halos(turn):
        @pl.when(here < count - 1)
        def _():
            halo(0, group_at(here + 1, turn), here + 1).start()

        @pl.when(here > 0)
        def _():
            group = group_at(here - 1, turn)
            halo(1, group, here - 1).start()
            halo(2, group, here - 1).start()

    ahead = 2
    for turn in range(ahead):
        send_halos(turn)

    @pl.when(here == 0)
    def _():
        xh[pl.ds(0, HALO), :] = jnp.zeros((HALO, channels), jnp.bfloat16)

    @pl.when(here == count - 1)
    def _():
        xh[pl.ds(rows + HALO, HALO), :] = jnp.zeros((HALO, channels), jnp.bfloat16)
        ch[pl.ds(rows, HALO), :] = jnp.zeros((HALO, channels), jnp.bfloat16)

    locals_[0].wait()
    locals_[1].wait()
    damping = 0.1 * jnp.mean(lv[...])

    @pl.loop(0, groups)
    def _(o):
        tile = pl.ds(pl.multiple_of(o * ROWS8, ROWS8), ROWS8)
        inverse = [1.0 / (lv[i, tile, :] + damping) for i in range(5)]
        basis = [[qv[j * 5 + i, tile, :] for i in range(5)] for j in range(5)]
        for at, (j, k) in enumerate(PAIRS):
            value = basis[j][0] * basis[k][0] * inverse[0]
            for i in range(1, 5):
                value = value + basis[j][i] * basis[k][i] * inverse[i]
            for h in range(per):
                ms[o * per + h, at] = value[h * lines:(h + 1) * lines].astype(jnp.bfloat16)

    def send_rows(step):
        target = lax.rem(here + step, count)
        return remote(ms.at[target], got_m.at[step], send_m.at[step], recv_m.at[step], target)

    got_m[0] = ms[here]
    locals_[2].wait()
    locals_[3].wait()

    @pl.loop(0, channels // LANES)
    def _(g):
        lanes = pl.ds(pl.multiple_of(g * LANES, LANES), LANES)
        for layer in range(layers):
            for k in range(TAPS):
                w_all[layer * TAPS + k, pl.ds(g, 1), :] = wv[layer, pl.ds(k, 1), lanes]
            w_all[layers * TAPS + layer, pl.ds(g, 1), :] = bv[pl.ds(layer, 1), lanes]

    into, back = token_permutation(False), token_permutation(True)
    keep = jnp.where(here > 0, 1.0, 0.0) * jnp.ones((ROWS8, LANES), jnp.float32)
    locals_[4].wait()
    locals_[5].wait()

    def gather_block(ref, at, base):
        return jnp.concatenate(
            [ref[pl.ds(at, HALO), pl.ds(pl.multiple_of(base + g * LANES, LANES), LANES)] for g in range(ROWS8)],
            axis=0)

    core, chip = lax.rem(here, 2), lax.div(here, 2)
    mate = here + 1 - 2 * core

    def to_mate(turn):
        return remote(gs.at[group_at(here, turn) * 2 + 1 - core], gm.at[turn], send_x.at[turn], recv_x.at[turn], mate)

    def to_owner(turn):
        return remote(fs.at[turn], got_g.at[chip], send_g.at[turn], recv_g.at[chip],
                      group_at(here, turn) * 2 + core)

    def written(group):
        return pltpu.make_async_copy(ot.at[:, lanes_of(group)], out_hbm.at[:, lanes_of(group)], store.at[group])

    @pl.loop(0, groups)
    def _(turn):
        group = group_at(here, turn)
        base = group * width
        tile = pl.ds(pl.multiple_of(group * ROWS8, ROWS8), ROWS8)

        @pl.when(turn < groups - ahead)
        def _():
            send_halos(turn + ahead)

        @pl.when(here > 0)
        def _():
            halo(0, group, here - 1).wait_recv()

        @pl.when(here < count - 1)
        def _():
            halo(1, group, here + 1).wait_recv()
            halo(2, group, here + 1).wait_recv()

        def arrange(source, target, blocks):
            wide = jnp.concatenate([gather_block(source, b * HALO, base) for b in range(blocks)], axis=1)
            moved = jnp.dot(into, wide, preferred_element_type=jnp.float32)
            for b in range(blocks):
                target[pl.ds(b * HALO, HALO)] = moved[:, b * LANES:(b + 1) * LANES].reshape(HALO, ROWS8, LANES)

        arrange(xh, x_all.at[0], rows // HALO + 2)
        arrange(ch, a_all.at[group], rows // HALO + 1)

        for layer in range(layers):
            forward_layer(layer, layers, rows, (rows + 3 * layers) // 2, tile, x_all, s_all, w_all, keep)
        @pl.when(turn > 0)
        def _():
            before = turn - 1
            to_mate(before).wait_recv()
            fs[before] = (gs[group_at(here, before) * 2 + core].astype(jnp.float32)
                          + gm[before].astype(jnp.float32)).astype(jnp.bfloat16)
            to_owner(before).start()

        for layer in reversed(range(layers)):
            backward_layer(layer, layers, rows, 16, tile, x_all, s_all, a_all.at[group], w_all, g_all,
                           dv_all.at[group])

        for h in range(per):
            for term in range(layers * 5):
                gs[group * per + h, term] = g_all[term, h * lines:(h + 1) * lines].astype(jnp.bfloat16)

        to_mate(turn).start()

        for part in range(4):
            @pl.when(turn * 4 + part + 1 < count)
            def _():
                send_rows(turn * 4 + part + 1).start()

    @pl.loop(1, count)
    def _(step):
        send_rows(step).wait()

    last = groups - 1
    to_mate(last).wait_recv()

    @pl.loop(1, groups)
    def _(step):
        source = lax.rem(chip + step, groups)
        remote(fs.at[0], got_g.at[source], send_g.at[0], recv_g.at[source], source * 2 + core).wait_recv()

    locals_[6].wait()
    total = gs[here].astype(jnp.float32) + gm[last].astype(jnp.float32)
    for step in range(1, groups):
        total = total + got_g[lax.rem(chip + step, groups)].astype(jnp.float32)
    total = total * scale
    order = {pair: i for i, pair in enumerate(PAIRS)}
    for layer in range(layers):
        slot = lax.rem(here - owner_ref[layer] + count, count)
        inverse = got_m[slot].astype(jnp.float32)
        for j in range(5):
            value = None
            for k in range(5):
                term = inverse[order[min(j, k), max(j, k)]] * total[layer * 5 + k]
                value = term if value is None else value + term
            for r in range(lines):
                part[j, pl.ds(layer, 1), r * LANES:(r + 1) * LANES] = value[r:r + 1]

    side, depth = lax.rem(lax.div(here, 2), 2), count // 4
    across = here + 2 - 4 * side

    def along(device, i):
        return lax.rem(device + 4 * i, count)

    def span_of(owner):
        return pl.ds(pl.multiple_of(owner * share, share), share)

    def pass_on(owner, target, slot):
        lanes = span_of(owner)
        return remote(full_p.at[:, :, lanes], full_p.at[:, :, lanes], send_p.at[slot], recv_p.at[owner], target)

    def score(owner):
        lanes = span_of(owner)
        both = []
        for j in range(5):
            value = full_p[j, :, lanes]
            high = value.astype(jnp.bfloat16).astype(jnp.float32)
            both.append(high + (value - high).astype(jnp.bfloat16).astype(jnp.float32))
        for e in range(tv.shape[0]):
            value = tv[e, 0, :, lanes].astype(jnp.float32) * both[0]
            for j in range(1, 5):
                value = value + tv[e, j, :, lanes].astype(jnp.float32) * both[j]
            sacc[e] = sacc[e] + value

    full_p[:, :, span_of(here)] = part[...]
    sends = []

    def send(owner, target):
        copy = pass_on(owner, target, len(sends))
        copy.start()
        sends.append(copy)

    def await_part(owner):
        pass_on(owner, mate, 0).wait_recv()

    for i in range(1, depth):
        send(here, along(here, i))
    send(here, across)
    send(here, mate)
    def put_back(group):
        blocks = rows // HALO
        tile = pl.ds(pl.multiple_of(group * ROWS8, ROWS8), ROWS8)
        taps = [w_all[k, tile, :] * 0.5 for k in range(TAPS)]
        pieces = []
        for b in range(blocks):
            dv = [dv_all[group, b * HALO + i] for i in range(HALO + TAPS - 1)]
            final_adjoint = [
                a_all[group, b * HALO + i]
                + ((taps[0] * dv[i] + taps[1] * dv[i + 1]) + (taps[2] * dv[i + 2] + taps[3] * dv[i + 3]))
                for i in range(HALO)
            ]
            pieces.append(jnp.concatenate(final_adjoint, axis=0).astype(jnp.bfloat16))
        moved = jnp.dot(back, jnp.concatenate(pieces, axis=1), preferred_element_type=jnp.float32)
        moved = moved.astype(jnp.bfloat16)
        for b in range(blocks):
            for g in range(ROWS8):
                lanes = pl.ds(pl.multiple_of(group * width + g * LANES, LANES), LANES)
                ot[pl.ds(b * HALO, HALO), lanes] = moved[g * HALO:(g + 1) * HALO, b * LANES:(b + 1) * LANES]
        written(group).start()

        @pl.when(here < count - 1)
        def _():
            halo(0, group, here + 1).wait_send()

        @pl.when(here > 0)
        def _():
            halo(1, group, here - 1).wait_send()
            halo(2, group, here - 1).wait_send()

    split = groups
    pl.loop(0, split)(put_back)
    sacc[...] = jnp.zeros_like(sacc)
    locals_[7].wait()
    score(here)
    for i in range(1, depth):
        await_part(along(here, i))
        send(along(here, i), across)
        send(along(here, i), mate)
    await_part(across)
    send(across, mate)
    pl.loop(split, groups)(put_back)
    for i in range(1, depth):
        score(along(here, i))
    for i in range(1, depth):
        await_part(along(across, i))
        send(along(across, i), mate)
    for i in range(depth):
        score(along(across, i))
    for owner in (mate, mate + 2 - 4 * side):
        for i in range(depth):
            await_part(along(owner, i))
            score(along(owner, i))

    for e in range(tv.shape[0]):
        rowed = jnp.sum(jnp.sum(sacc[e], axis=0, keepdims=True), axis=1, keepdims=True)
        p_ref[pl.ds(e, 1), :] = jnp.broadcast_to(rowed * final, (1, LANES))

    @pl.loop(0, groups)
    def _(i):
        written(i).wait()

    for copy in sends:
        copy.wait_send()

    @pl.loop(0, last)
    def _(turn):
        to_mate(turn).wait_send()
        to_owner(turn).wait_send()

    to_mate(last).wait_send()


def fused(acts, cots, weights, bias, owner_map, basis, vals, train, scale, final):
    rows, channels = acts.shape
    layers = weights.shape[0]
    count = lax.axis_size("dp")
    share = channels // count
    lines = share // LANES
    groups = channels // (ROWS8 * LANES)
    held = rows + 2 * HALO
    vmem = pl.BlockSpec(memory_space=pltpu.VMEM)
    anywhere = pl.BlockSpec(memory_space=pltpu.HBM)
    dma = pltpu.SemaphoreType.DMA
    f32, b16 = jnp.float32, jnp.bfloat16
    tall = channels // LANES
    return pl.pallas_call(
        functools.partial(fused_kernel, count, layers, rows, channels, scale, final),
        out_shape=(
            jax.ShapeDtypeStruct((rows, channels), b16),
            jax.ShapeDtypeStruct((train.shape[0], LANES), f32),
        ),
        in_specs=[anywhere] * 8,
        out_specs=(anywhere, vmem),
        scratch_shapes=[
            pltpu.VMEM((held, channels), b16),
            pltpu.VMEM((rows + HALO, channels), b16),
            pltpu.VMEM(weights.shape, f32),
            pltpu.VMEM(bias.shape, f32),
            pltpu.VMEM((25, tall, LANES), f32),
            pltpu.VMEM((5, tall, LANES), f32),
            pltpu.VMEM((layers * 5, tall, LANES), f32),
            pltpu.VMEM((layers, held, ROWS8, LANES), f32),
            pltpu.VMEM((layers, held, ROWS8, LANES), f32),
            pltpu.VMEM((groups, rows + HALO, ROWS8, LANES), f32),
            pltpu.VMEM((layers * 5, ROWS8, LANES), f32),
            pltpu.VMEM((groups, rows + ROWS8, ROWS8, LANES), f32),
            pltpu.VMEM((rows, channels), b16),
            pltpu.VMEM((count, len(PAIRS), lines, LANES), b16),
            pltpu.VMEM((count, len(PAIRS), lines, LANES), b16),
            pltpu.VMEM((count, layers * 5, lines, LANES), b16),
            pltpu.VMEM((groups, layers * 5, lines, LANES), b16),
            pltpu.VMEM((groups, layers * 5, lines, LANES), b16),
            pltpu.VMEM((groups, layers * 5, lines, LANES), b16),
            pltpu.VMEM((5, layers, share), f32),
            pltpu.VMEM((5, layers, channels), f32),
            pltpu.VMEM(train.shape, b16),
            pltpu.VMEM((train.shape[0], layers, share), f32),
            pltpu.SMEM(owner_map.shape, owner_map.dtype),
            dma((8,)), dma((groups,)),
            dma((3, groups)), dma((3, groups)),
            dma((count,)), dma((count,)), dma((groups,)), dma((groups,)), dma((groups,)), dma((groups,)),
            dma((count,)), dma((count,)),
        ],
        compiler_params=pltpu.CompilerParams(
            collective_id=0, has_side_effects=True, vmem_limit_bytes=63 << 20),
    )(owner_map, acts, cots, weights, bias, basis.reshape(25, tall, LANES), vals.reshape(5, tall, LANES), train)


def finish_kernel(pieces, a_hbm, v_hbm, i_hbm, out_hbm, s_hbm, held, v_ref, i_ref, s_ref, load, store, small):
    width = a_hbm.shape[0] // pieces
    slabs = [pl.ds(i * width, width) for i in range(pieces)]
    reads = [pltpu.make_async_copy(a_hbm.at[slab, :], held.at[slab, :], load.at[i]) for i, slab in enumerate(slabs)]
    writes = [pltpu.make_async_copy(held.at[slab, :], out_hbm.at[slab, :], store.at[i])
              for i, slab in enumerate(slabs)]
    loads = [pltpu.make_async_copy(v_hbm, v_ref, small.at[0]), pltpu.make_async_copy(i_hbm, i_ref, small.at[1])]
    for copy in reads + loads:
        copy.start()
    for copy, onward in zip(reads, writes):
        copy.wait()
        onward.start()
    for copy in loads:
        copy.wait()
    examples = v_ref.shape[0]
    picks = i_ref.shape[1]
    local = i_ref[...] - lax.axis_index("dp") * examples
    chosen = jnp.broadcast_to(local, (examples, picks)) == lax.broadcasted_iota(jnp.int32, (examples, picks), 0)
    s_ref[...] = jnp.sum(jnp.where(chosen, v_ref[:, :picks], 0.0), axis=0, keepdims=True)
    picked = pltpu.make_async_copy(s_ref, s_hbm, small.at[2])
    picked.start()
    for copy in writes:
        copy.wait()
    picked.wait()


def finish(moved, values, batch_index):
    picks = batch_index.shape[0]
    pieces = 8
    anywhere = pl.BlockSpec(memory_space=pltpu.HBM)
    return pl.pallas_call(
        functools.partial(finish_kernel, pieces),
        out_shape=(
            jax.ShapeDtypeStruct(moved.shape, moved.dtype),
            jax.ShapeDtypeStruct((1, picks), jnp.float32),
        ),
        in_specs=[anywhere] * 3,
        out_specs=(anywhere, anywhere),
        scratch_shapes=[
            pltpu.VMEM(moved.shape, moved.dtype),
            pltpu.VMEM(values.shape, values.dtype),
            pltpu.VMEM((1, picks), batch_index.dtype),
            pltpu.VMEM((1, picks), jnp.float32),
            pltpu.SemaphoreType.DMA((pieces,)),
            pltpu.SemaphoreType.DMA((pieces,)),
            pltpu.SemaphoreType.DMA((3,)),
        ],
        compiler_params=pltpu.CompilerParams(vmem_limit_bytes=63 << 20),
    )(moved, values, batch_index.reshape(1, picks))


def precondition_apart(query_acts, cotangent, conv_weight, conv_bias, owner_map, basis_store, lambda_store,
                       norm_scale):
    rows, channels = query_acts.shape
    layers = conv_weight.shape[0]
    here = lax.axis_index("dp")
    before = shifted(query_acts[rows - HALO_ROWS:], "dp", 1)
    after = shifted(jnp.concatenate([query_acts[:HALO_ROWS], cotangent[:HALO_ROWS]]), "dp", -1)
    halo_acts = jnp.concatenate([before, after[:HALO_ROWS]])
    halo_cots = jnp.concatenate([jnp.zeros_like(before), after[HALO_ROWS:]])
    own_rows = inverse_rows(basis_store[0], lambda_store[0])
    adjoint, partial = window(query_acts, cotangent, halo_acts, halo_cots, conv_weight, conv_bias)
    held = jnp.where((owner_map == here)[:, None, None], own_rows[None], 0.0)
    inverse = lax.psum(held, "dp")
    summed = (lax.psum(partial, "dp") * norm_scale).reshape(layers, 5, channels)
    order = {pair: i for i, pair in enumerate(PAIRS)}
    everyone = jnp.stack([
        sum(inverse[:, order[min(j, k), max(j, k)]] * summed[:, k] for k in range(5))
        for j in range(5)
    ], axis=1)
    return adjoint, everyone


def on_device(query_acts, cotangent, conv_weight, conv_bias, owner_map, basis_store, lambda_store,
              train_grads, batch_index):
    rows, channels = query_acts.shape
    layers = conv_weight.shape[0]
    count = lax.axis_size("dp")
    here = lax.axis_index("dp")
    norm_scale = 1.0 / math.sqrt(rows * count)
    lines = channels // (LANES * count)
    examples = train_grads.shape[0]
    final = 1.0 / math.sqrt(5 * layers * channels)
    if lines == 4 and count % 4 == 0 and channels == lines * LANES * count and (
            rows % HALO == 0 and batch_index.shape[0] <= LANES):
        moved, values = fused(query_acts, cotangent, conv_weight, conv_bias, owner_map, basis_store[0],
                                lambda_store[0], train_grads.transpose(0, 2, 1, 3), norm_scale, final)
        adjoint, scores = finish(moved, values, batch_index)
        return (adjoint, scores.reshape(-1))
    else:
        adjoint, everyone = precondition_apart(query_acts, cotangent, conv_weight, conv_bias, owner_map,
                                               basis_store, lambda_store, norm_scale)
        high = everyone.astype(jnp.bfloat16)
        low = (everyone - high.astype(jnp.float32)).astype(jnp.bfloat16)
        both = high.astype(jnp.float32) + low.astype(jnp.float32)
        values = jnp.sum(train_grads.astype(jnp.float32) * both[None], axis=(1, 2, 3)) * final
    local_index = batch_index - here * examples
    chosen = local_index[:, None] == jnp.arange(examples, dtype=jnp.int32)[None, :]
    scores = jnp.sum(jnp.where(chosen, values[None, :], 0.0), axis=1)
    return (adjoint, scores)


def solution(mesh):
    in_specs = (
        P(("groups", "dp"), None),
        P(("groups", "dp"), None),
        P(),
        P(),
        P(),
        P("dp", None, None),
        P("dp", None, None),
        P(("groups", "dp"), None, None, None),
        P(("groups", "dp")),
    )
    out_specs = (P(("groups", "dp"), None), P(("groups", "dp")))
    return jax.shard_map(
        on_device, mesh=mesh, in_specs=in_specs, out_specs=out_specs, check_vma=False
    )
```

```python
import functools
import math

import jax
import jax.numpy as jnp
import numpy as np
from jax import lax
from jax.experimental import pallas as pl
from jax.experimental.pallas import tpu as pltpu
from jax.sharding import PartitionSpec as P

LANES = 128
SUB = 8
TAPS = 4
HALO_ROWS = 16
PAIRS = [(j, k) for j in range(5) for k in range(j, 5)]


def layout_plan(rows, layers):
    reach = (TAPS - 1) * layers
    extended = rows + 2 * reach
    fold = -(-extended // SUB)
    padded = -(-(fold * SUB) // 16) * 16
    return reach, fold, padded


def permutations(rows, layers):
    reach, fold, padded = layout_plan(rows, layers)
    columns = rows + 2 * HALO_ROWS
    into = np.zeros((padded, columns), np.float32)
    back = np.zeros((rows, padded), np.float32)
    for j in range(fold):
        for s in range(SUB):
            token = fold * s + j - reach
            row = SUB * j + s
            if 0 <= token < rows:
                into[row, token] = 1.0
                back[token, row] = 1.0
            elif -reach <= token < 0:
                into[row, rows + HALO_ROWS + token] = 1.0
            elif rows <= token < rows + reach:
                into[row, HALO_ROWS + token] = 1.0
    return jnp.asarray(into, jnp.bfloat16), jnp.asarray(back, jnp.bfloat16)


def rounded(value):
    return value.astype(jnp.bfloat16).astype(jnp.float32)


def window_chunk(lanes, rows, layers, is_first, w_ref, b_ref, x_all, c_all, slope_all, g_ref):
    reach, fold, padded = layout_plan(rows, layers)
    sub = lax.broadcasted_iota(jnp.int32, (SUB, LANES), 0)
    edges = {}

    def own(j, low, high):
        tokens = [fold * s + j - reach for s in range(SUB)]
        inside = tuple(low <= t < high for t in tokens)
        if all(inside):
            return None
        if inside not in edges:
            lead = next(i for i, ok in enumerate(inside) if ok)
            tail = max(i for i, ok in enumerate(inside) if ok)
            edges[inside] = (sub >= lead) & (sub <= tail)
        return edges[inside]

    zero = jnp.zeros((SUB, LANES), jnp.float32)

    def keep(value, mask):
        return value if mask is None else jnp.where(mask, value, zero)

    def row(ref, *at):
        return jnp.broadcast_to(ref[at[:-1] + (pl.ds(at[-1], 1), lanes)], (SUB, LANES))

    live = {}

    def begun(j):
        mask = own(j, 0, 1 << 30)
        if mask is None:
            return None
        key = id(mask)
        if key not in live:
            live[key] = mask | jnp.logical_not(is_first)
        return live[key]

    last = TAPS - 1
    for layer in range(layers):
        taps = [row(w_ref, layer, k) * 0.5 for k in range(TAPS)]
        bias = row(b_ref, layer) * 0.5
        base = layer * (fold + last) * SUB
        for i in range(last):
            wrapped = x_all[pl.ds(base + (fold + i) * SUB, SUB), lanes]
            x_all[pl.ds(base + i * SUB, SUB), lanes] = pltpu.roll(wrapped, 1, 0)
        x = [x_all[pl.ds(base + i * SUB, SUB), lanes] for i in range(fold + last)]
        following = base + (fold + last + last) * SUB
        for j in range(fold):
            half = bias
            for k in range(TAPS):
                half = half + taps[k] * x[last + j - k]
            bent = jnp.tanh(half)
            up = 1.0 + bent
            slope_all[pl.ds((layer * fold + j) * SUB, SUB), lanes] = up * (1.0 + half * (1.0 - bent))
            if layer < layers - 1:
                fresh = keep(rounded(x[last + j] + half * up), begun(j))
                x_all[pl.ds(following + j * SUB, SUB), lanes] = fresh
    for layer in reversed(range(layers)):
        taps = [row(w_ref, layer, k) * 0.5 for k in range(TAPS)]
        base = layer * (fold + last) * SUB
        doubled = [None] * (fold + last)
        sums = [zero] * (TAPS + 1)

        def at(i):
            return x_all[pl.ds(base + i * SUB, SUB), lanes]

        for j in range(fold):
            adjoint = c_all[pl.ds(j * SUB, SUB), lanes]
            slope = slope_all[pl.ds((layer * fold + j) * SUB, SUB), lanes]
            grad = keep(rounded(adjoint * slope), own(j, 0, 1 << 30))
            doubled[j] = grad
            if j < last:
                doubled[fold + j] = pltpu.roll(grad, SUB - 1, 0)
            inner = keep(grad, own(j, -(1 << 30), rows))
            for k in range(TAPS):
                sums[k] = sums[k] + at(last + j - k) * inner
            sums[TAPS] = sums[TAPS] + inner
        for j in range(fold):
            total = c_all[pl.ds(j * SUB, SUB), lanes]
            back = taps[0] * doubled[j]
            for k in range(1, TAPS):
                back = back + taps[k] * doubled[j + k]
            c_all[pl.ds(j * SUB, SUB), lanes] = rounded(total + back)
        for k in range(TAPS + 1):
            g_ref[pl.ds(layer * 5 + k, 1), lanes] = 0.5 * jnp.sum(sums[k], axis=0, keepdims=True)


def window_kernel(rows, layers, x_ref, c_ref, hx_ref, hc_ref, w_ref, b_ref, into_ref, back_ref,
                  out_ref, g_ref, x_all, c_all, slope_all):
    reach, fold, padded = layout_plan(rows, layers)
    width = x_ref.shape[1]
    is_first = lax.axis_index("dp") == 0
    count = fold * SUB
    acts = jnp.concatenate([x_ref[...], hx_ref[...]], axis=0)
    cots = jnp.concatenate([c_ref[...], hc_ref[...]], axis=0)
    x_all[pl.ds((TAPS - 1) * SUB, count), :] = jnp.dot(
        into_ref[...], acts, preferred_element_type=jnp.float32)[:count]
    c_all[...] = jnp.dot(into_ref[...], cots, preferred_element_type=jnp.float32)

    @pl.loop(0, width // LANES)
    def _(chunk):
        lanes = pl.ds(pl.multiple_of(chunk * LANES, LANES), LANES)
        window_chunk(lanes, rows, layers, is_first, w_ref, b_ref, x_all, c_all, slope_all, g_ref)

    out_ref[...] = jnp.dot(
        back_ref[...], c_all[...].astype(jnp.bfloat16), preferred_element_type=jnp.float32
    ).astype(jnp.bfloat16)


def window(acts, cots, halo_acts, halo_cots, weights, bias):
    rows, channels = acts.shape
    layers = weights.shape[0]
    reach, fold, padded = layout_plan(rows, layers)
    width = 512
    into, back = permutations(rows, layers)
    block = lambda *lead: pl.BlockSpec(lead + (width,), lambda i: (0,) * len(lead) + (i,))
    whole = lambda a: pl.BlockSpec(a.shape, lambda i: (0, 0))
    return pl.pallas_call(
        functools.partial(window_kernel, rows, layers),
        grid=(channels // width,),
        out_shape=(
            jax.ShapeDtypeStruct((rows, channels), jnp.bfloat16),
            jax.ShapeDtypeStruct((layers * 5, channels), jnp.float32),
        ),
        in_specs=[
            block(rows), block(rows), block(2 * HALO_ROWS), block(2 * HALO_ROWS),
            block(layers, TAPS), block(layers), whole(into), whole(back),
        ],
        out_specs=(block(rows), block(layers * 5)),
        scratch_shapes=[
            pltpu.VMEM((layers * (fold + TAPS - 1) * SUB, width), jnp.float32),
            pltpu.VMEM((padded, width), jnp.float32),
            pltpu.VMEM((layers * fold * SUB, width), jnp.float32),
        ],
        compiler_params=pltpu.CompilerParams(vmem_limit_bytes=24 << 20),
        cost_estimate=pl.CostEstimate(flops=200_000_000, bytes_accessed=10_000_000, transcendentals=5_000_000),
    )(acts, cots, halo_acts, halo_cots, weights, bias, into, back)


def shifted(value, axis, steps):
    count = lax.axis_size(axis)
    first, final = (max(0, -steps), min(count, count - steps))
    return lax.ppermute(value, axis, [(s, s + steps) for s in range(first, final)])


def inverse_rows(basis, vals):
    channels = basis.shape[-1]
    blocks = basis.reshape(5, 5, channels)
    scale = 1.0 / (vals + 0.1 * jnp.mean(vals))
    return jnp.stack([jnp.sum(blocks[j] * blocks[k] * scale, axis=0) for j, k in PAIRS])


ROWS8 = 8
HALO = 16


def token_permutation(invert):
    row = lax.broadcasted_iota(jnp.int32, (LANES, LANES), 0)
    col = lax.broadcasted_iota(jnp.int32, (LANES, LANES), 1)
    if invert:
        row, col = col, row
    same = ((row >> 3) == (col & 15)) & ((row & 7) == (col >> 4))
    return jnp.where(same, 1.0, 0.0).astype(jnp.bfloat16)


def forward_layer(layer, layers, rows, step, tile, x_all, s_all, w_all, keep):
    taps = [w_all[layer * TAPS + k, tile, :] * 0.5 for k in range(TAPS)]
    bias = w_all[layers * TAPS + layer, tile, :] * 0.5

    def span(first, n, mask=None):
        x = [x_all[layer, first - 3 + i] for i in range(n + 3)]
        for i in range(n):
            half = ((taps[0] * x[i + 3] + taps[1] * x[i + 2]) + (taps[2] * x[i + 1] + taps[3] * x[i])) + bias
            bent = jnp.tanh(half)
            up = 1.0 + bent
            gain = half * up
            s_all[layer, first + i] = up + gain * (1.0 - bent)
            if layer < layers - 1:
                fresh = x[i + 3] + gain
                x_all[layer + 1, first + i] = fresh if mask is None else fresh * mask

    early = 3 * (layers - 1 - layer)
    if early:
        span(HALO - early, early, keep)
    total = rows + 3 * layers
    full, rest = total // step, total % step

    @pl.loop(0, full)
    def _(j):
        span(HALO + j * step, step)

    if rest:
        span(HALO + full * step, rest)


def pairwise(values):
    while len(values) > 1:
        values = [values[i] + values[i + 1] if i + 1 < len(values) else values[i]
                  for i in range(0, len(values), 2)]
    return values[0]


def backward_layer(layer, layers, rows, step, tile, x_all, s_all, a_all, w_all, g_all, dv_all):
    taps = [w_all[layer * TAPS + k, tile, :] * 0.5 for k in range(TAPS)]

    def grads(first, n):
        return [a_all[first + i] * s_all[layer, HALO + first + i] for i in range(n)]

    def back(first, dv, n):
        for i in range(n):
            a_all[first + i] = a_all[first + i] + (
                (taps[0] * dv[i] + taps[1] * dv[i + 1]) + (taps[2] * dv[i + 2] + taps[3] * dv[i + 3]))

    def sums(first, dv, n):
        x = [x_all[layer, HALO + first - 3 + i] for i in range(n + 3)]
        terms = [pairwise([x[i + 3 - k] * dv[i] for i in range(n)]) for k in range(TAPS)]
        return terms + [pairwise(dv[:n])]

    def body(j, carry):
        first = j * step
        dv = list(carry[:3]) + grads(first + 3, step)
        part = sums(first, dv, step)
        if layer:
            back(first, dv, step)
        else:
            keep_grads(first + 3, dv[3:])
        return tuple(dv[step:step + 3]) + tuple(a + b for a, b in zip(carry[3:], part))

    def keep_grads(first, dv):
        for i, value in enumerate(dv):
            dv_all[first + i] = value

    zero = jnp.zeros((ROWS8, LANES), jnp.float32)
    early = grads(0, 3)
    if not layer:
        keep_grads(0, early)
    carry = lax.fori_loop(0, rows // step, body, tuple(early) + (zero,) * (TAPS + 1))
    for k in range(TAPS + 1):
        g_all[layer * 5 + k] = 0.5 * carry[3 + k]
    extra = 3 * layer
    if extra:
        dv = list(carry[:3]) + grads(rows + 3, extra)
        back(rows, dv, extra)


def fused_kernel(count, layers, rows, channels, scale, final, o_hbm, x_hbm, c_hbm, w_hbm, b_hbm, q_hbm, l_hbm, t_hbm,
                 out_hbm, p_ref, xh, ch, wv, bv, qv, lv, w_all, x_all, s_all, a_all, g_all, dv_all, ot,
                 ms, got_m, gs, gm, fs, got_g, part, full_p, tv, sacc, owner_ref,
                 load, store, send_h, recv_h, send_m, recv_m, send_x, recv_x, send_g, recv_g, send_p, recv_p):
    here = lax.axis_index("dp")
    width = ROWS8 * LANES
    groups = channels // width
    share = channels // count
    lines = share // LANES
    per = ROWS8 // lines

    def remote(source, target_ref, sent, got, device):
        return pltpu.make_async_remote_copy(
            src_ref=source, dst_ref=target_ref, send_sem=sent, recv_sem=got,
            device_id={"dp": device}, device_id_type=pl.DeviceIdType.MESH)

    locals_ = [
        pltpu.make_async_copy(q_hbm, qv, load.at[0]),
        pltpu.make_async_copy(l_hbm, lv, load.at[1]),
        pltpu.make_async_copy(w_hbm, wv, load.at[2]),
        pltpu.make_async_copy(b_hbm, bv, load.at[3]),
        pltpu.make_async_copy(x_hbm, xh.at[pl.ds(HALO, rows), :], load.at[4]),
        pltpu.make_async_copy(c_hbm, ch.at[pl.ds(0, rows), :], load.at[5]),
        pltpu.make_async_copy(o_hbm, owner_ref, load.at[6]),
        pltpu.make_async_copy(t_hbm, tv, load.at[7]),
    ]
    for copy in locals_:
        copy.start()
    barrier = pltpu.get_barrier_semaphore()

    @pl.loop(1, count)
    def _(step):
        pl.semaphore_signal(barrier, inc=1, device_id={"dp": lax.rem(here + step, count)},
                            device_id_type=pl.DeviceIdType.MESH)

    pl.semaphore_wait(barrier, count - 1)

    def lanes_of(group):
        return pl.ds(pl.multiple_of(group * width, width), width)

    def group_at(device, i):
        return lax.rem(lax.div(device, per) + 1 + i, groups)

    def halo(kind, group, device):
        lanes = lanes_of(group)
        if kind == 0:
            source, target = x_hbm.at[pl.ds(rows - HALO, HALO), lanes], xh.at[pl.ds(0, HALO), lanes]
        elif kind == 1:
            source, target = x_hbm.at[pl.ds(0, HALO), lanes], xh.at[pl.ds(rows + HALO, HALO), lanes]
        else:
            source, target = c_hbm.at[pl.ds(0, HALO), lanes], ch.at[pl.ds(rows, HALO), lanes]
        return remote(source, target, send_h.at[kind, group], recv_h.at[kind, group], device)

    def send_halos(turn):
        @pl.when(here < count - 1)
        def _():
            halo(0, group_at(here + 1, turn), here + 1).start()

        @pl.when(here > 0)
        def _():
            group = group_at(here - 1, turn)
            halo(1, group, here - 1).start()
            halo(2, group, here - 1).start()

    ahead = 2
    for turn in range(ahead):
        send_halos(turn)

    @pl.when(here == 0)
    def _():
        xh[pl.ds(0, HALO), :] = jnp.zeros((HALO, channels), jnp.bfloat16)

    @pl.when(here == count - 1)
    def _():
        xh[pl.ds(rows + HALO, HALO), :] = jnp.zeros((HALO, channels), jnp.bfloat16)
        ch[pl.ds(rows, HALO), :] = jnp.zeros((HALO, channels), jnp.bfloat16)

    locals_[0].wait()
    locals_[1].wait()
    damping = 0.1 * jnp.mean(lv[...])

    @pl.loop(0, groups)
    def _(o):
        tile = pl.ds(pl.multiple_of(o * ROWS8, ROWS8), ROWS8)
        inverse = [1.0 / (lv[i, tile, :] + damping) for i in range(5)]
        basis = [[qv[j * 5 + i, tile, :] for i in range(5)] for j in range(5)]
        for at, (j, k) in enumerate(PAIRS):
            value = basis[j][0] * basis[k][0] * inverse[0]
            for i in range(1, 5):
                value = value + basis[j][i] * basis[k][i] * inverse[i]
            for h in range(per):
                ms[o * per + h, at] = value[h * lines:(h + 1) * lines].astype(jnp.bfloat16)

    def send_rows(step):
        target = lax.rem(here + step, count)
        return remote(ms.at[target], got_m.at[step], send_m.at[step], recv_m.at[step], target)

    got_m[0] = ms[here]
    locals_[2].wait()
    locals_[3].wait()

    @pl.loop(0, channels // LANES)
    def _(g):
        lanes = pl.ds(pl.multiple_of(g * LANES, LANES), LANES)
        for layer in range(layers):
            for k in range(TAPS):
                w_all[layer * TAPS + k, pl.ds(g, 1), :] = wv[layer, pl.ds(k, 1), lanes]
            w_all[layers * TAPS + layer, pl.ds(g, 1), :] = bv[pl.ds(layer, 1), lanes]

    into, back = token_permutation(False), token_permutation(True)
    keep = jnp.where(here > 0, 1.0, 0.0) * jnp.ones((ROWS8, LANES), jnp.float32)
    locals_[4].wait()
    locals_[5].wait()

    def gather_block(ref, at, base):
        return jnp.concatenate(
            [ref[pl.ds(at, HALO), pl.ds(pl.multiple_of(base + g * LANES, LANES), LANES)] for g in range(ROWS8)],
            axis=0)

    core, chip = lax.rem(here, 2), lax.div(here, 2)
    mate = here + 1 - 2 * core

    def to_mate(turn):
        return remote(gs.at[group_at(here, turn) * 2 + 1 - core], gm.at[turn], send_x.at[turn], recv_x.at[turn], mate)

    def to_owner(turn):
        return remote(fs.at[turn], got_g.at[chip], send_g.at[turn], recv_g.at[chip],
                      group_at(here, turn) * 2 + core)

    def written(group):
        return pltpu.make_async_copy(ot.at[:, lanes_of(group)], out_hbm.at[:, lanes_of(group)], store.at[group])

    @pl.loop(0, groups)
    def _(turn):
        group = group_at(here, turn)
        base = group * width
        tile = pl.ds(pl.multiple_of(group * ROWS8, ROWS8), ROWS8)

        @pl.when(turn < groups - ahead)
        def _():
            send_halos(turn + ahead)

        @pl.when(here > 0)
        def _():
            halo(0, group, here - 1).wait_recv()

        @pl.when(here < count - 1)
        def _():
            halo(1, group, here + 1).wait_recv()
            halo(2, group, here + 1).wait_recv()

        def arrange(source, target, blocks):
            wide = jnp.concatenate([gather_block(source, b * HALO, base) for b in range(blocks)], axis=1)
            moved = jnp.dot(into, wide, preferred_element_type=jnp.float32)
            for b in range(blocks):
                target[pl.ds(b * HALO, HALO)] = moved[:, b * LANES:(b + 1) * LANES].reshape(HALO, ROWS8, LANES)

        arrange(xh, x_all.at[0], rows // HALO + 2)
        arrange(ch, a_all.at[group], rows // HALO + 1)

        for layer in range(layers):
            forward_layer(layer, layers, rows, (rows + 3 * layers) // 2, tile, x_all, s_all, w_all, keep)
        @pl.when(turn > 0)
        def _():
            before = turn - 1
            to_mate(before).wait_recv()
            fs[before] = (gs[group_at(here, before) * 2 + core].astype(jnp.float32)
                          + gm[before].astype(jnp.float32)).astype(jnp.bfloat16)
            to_owner(before).start()

        for layer in reversed(range(layers)):
            backward_layer(layer, layers, rows, 32, tile, x_all, s_all, a_all.at[group], w_all, g_all,
                           dv_all.at[group])

        for h in range(per):
            for term in range(layers * 5):
                gs[group * per + h, term] = g_all[term, h * lines:(h + 1) * lines].astype(jnp.bfloat16)

        to_mate(turn).start()

        for part in range(4):
            @pl.when(turn * 4 + part + 1 < count)
            def _():
                send_rows(turn * 4 + part + 1).start()

    @pl.loop(1, count)
    def _(step):
        send_rows(step).wait()

    last = groups - 1
    to_mate(last).wait_recv()

    @pl.loop(1, groups)
    def _(step):
        source = lax.rem(chip + step, groups)
        remote(fs.at[0], got_g.at[source], send_g.at[0], recv_g.at[source], source * 2 + core).wait_recv()

    locals_[6].wait()
    total = gs[here].astype(jnp.float32) + gm[last].astype(jnp.float32)
    for step in range(1, groups):
        total = total + got_g[lax.rem(chip + step, groups)].astype(jnp.float32)
    total = total * scale
    order = {pair: i for i, pair in enumerate(PAIRS)}
    for layer in range(layers):
        slot = lax.rem(here - owner_ref[layer] + count, count)
        inverse = got_m[slot].astype(jnp.float32)
        for j in range(5):
            value = None
            for k in range(5):
                term = inverse[order[min(j, k), max(j, k)]] * total[layer * 5 + k]
                value = term if value is None else value + term
            for r in range(lines):
                part[j, pl.ds(layer, 1), r * LANES:(r + 1) * LANES] = value[r:r + 1]

    side, depth = lax.rem(lax.div(here, 2), 2), count // 4
    across = here + 2 - 4 * side

    def along(device, i):
        return lax.rem(device + 4 * i, count)

    def span_of(owner):
        return pl.ds(pl.multiple_of(owner * share, share), share)

    def pass_on(owner, target, slot):
        lanes = span_of(owner)
        return remote(full_p.at[:, :, lanes], full_p.at[:, :, lanes], send_p.at[slot], recv_p.at[owner], target)

    def score(owner):
        lanes = span_of(owner)
        both = []
        for j in range(5):
            value = full_p[j, :, lanes]
            high = value.astype(jnp.bfloat16).astype(jnp.float32)
            both.append(high + (value - high).astype(jnp.bfloat16).astype(jnp.float32))
        for e in range(tv.shape[0]):
            value = tv[e, 0, :, lanes].astype(jnp.float32) * both[0]
            for j in range(1, 5):
                value = value + tv[e, j, :, lanes].astype(jnp.float32) * both[j]
            sacc[e] = sacc[e] + value

    full_p[:, :, span_of(here)] = part[...]
    sends = []

    def send(owner, target):
        copy = pass_on(owner, target, len(sends))
        copy.start()
        sends.append(copy)

    def await_part(owner):
        pass_on(owner, mate, 0).wait_recv()

    for i in range(1, depth):
        send(here, along(here, i))
    send(here, across)
    send(here, mate)
    def put_back(group):
        blocks = rows // HALO
        tile = pl.ds(pl.multiple_of(group * ROWS8, ROWS8), ROWS8)
        taps = [w_all[k, tile, :] * 0.5 for k in range(TAPS)]
        pieces = []
        for b in range(blocks):
            dv = [dv_all[group, b * HALO + i] for i in range(HALO + TAPS - 1)]
            final_adjoint = [
                a_all[group, b * HALO + i]
                + ((taps[0] * dv[i] + taps[1] * dv[i + 1]) + (taps[2] * dv[i + 2] + taps[3] * dv[i + 3]))
                for i in range(HALO)
            ]
            pieces.append(jnp.concatenate(final_adjoint, axis=0).astype(jnp.bfloat16))
        moved = jnp.dot(back, jnp.concatenate(pieces, axis=1), preferred_element_type=jnp.float32)
        moved = moved.astype(jnp.bfloat16)
        for b in range(blocks):
            for g in range(ROWS8):
                lanes = pl.ds(pl.multiple_of(group * width + g * LANES, LANES), LANES)
                ot[pl.ds(b * HALO, HALO), lanes] = moved[g * HALO:(g + 1) * HALO, b * LANES:(b + 1) * LANES]
        written(group).start()

        @pl.when(here < count - 1)
        def _():
            halo(0, group, here + 1).wait_send()

        @pl.when(here > 0)
        def _():
            halo(1, group, here - 1).wait_send()
            halo(2, group, here - 1).wait_send()

    split = groups
    pl.loop(0, split)(put_back)
    sacc[...] = jnp.zeros_like(sacc)
    locals_[7].wait()
    score(here)
    for i in range(1, depth):
        await_part(along(here, i))
        send(along(here, i), across)
        send(along(here, i), mate)
    await_part(across)
    send(across, mate)
    pl.loop(split, groups)(put_back)
    for i in range(1, depth):
        score(along(here, i))
    for i in range(1, depth):
        await_part(along(across, i))
        send(along(across, i), mate)
    for i in range(depth):
        score(along(across, i))
    for owner in (mate, mate + 2 - 4 * side):
        for i in range(depth):
            await_part(along(owner, i))
            score(along(owner, i))

    for e in range(tv.shape[0]):
        rowed = jnp.sum(jnp.sum(sacc[e], axis=0, keepdims=True), axis=1, keepdims=True)
        p_ref[pl.ds(e, 1), :] = jnp.broadcast_to(rowed * final, (1, LANES))

    @pl.loop(0, groups)
    def _(i):
        written(i).wait()

    for copy in sends:
        copy.wait_send()

    @pl.loop(0, last)
    def _(turn):
        to_mate(turn).wait_send()
        to_owner(turn).wait_send()

    to_mate(last).wait_send()


def fused(acts, cots, weights, bias, owner_map, basis, vals, train, scale, final):
    rows, channels = acts.shape
    layers = weights.shape[0]
    count = lax.axis_size("dp")
    share = channels // count
    lines = share // LANES
    groups = channels // (ROWS8 * LANES)
    held = rows + 2 * HALO
    vmem = pl.BlockSpec(memory_space=pltpu.VMEM)
    anywhere = pl.BlockSpec(memory_space=pltpu.HBM)
    dma = pltpu.SemaphoreType.DMA
    f32, b16 = jnp.float32, jnp.bfloat16
    tall = channels // LANES
    return pl.pallas_call(
        functools.partial(fused_kernel, count, layers, rows, channels, scale, final),
        out_shape=(
            jax.ShapeDtypeStruct((rows, channels), b16),
            jax.ShapeDtypeStruct((train.shape[0], LANES), f32),
        ),
        in_specs=[anywhere] * 8,
        out_specs=(anywhere, vmem),
        scratch_shapes=[
            pltpu.VMEM((held, channels), b16),
            pltpu.VMEM((rows + HALO, channels), b16),
            pltpu.VMEM(weights.shape, f32),
            pltpu.VMEM(bias.shape, f32),
            pltpu.VMEM((25, tall, LANES), f32),
            pltpu.VMEM((5, tall, LANES), f32),
            pltpu.VMEM((layers * 5, tall, LANES), f32),
            pltpu.VMEM((layers, held, ROWS8, LANES), f32),
            pltpu.VMEM((layers, held, ROWS8, LANES), f32),
            pltpu.VMEM((groups, rows + HALO, ROWS8, LANES), f32),
            pltpu.VMEM((layers * 5, ROWS8, LANES), f32),
            pltpu.VMEM((groups, rows + ROWS8, ROWS8, LANES), f32),
            pltpu.VMEM((rows, channels), b16),
            pltpu.VMEM((count, len(PAIRS), lines, LANES), b16),
            pltpu.VMEM((count, len(PAIRS), lines, LANES), b16),
            pltpu.VMEM((count, layers * 5, lines, LANES), b16),
            pltpu.VMEM((groups, layers * 5, lines, LANES), b16),
            pltpu.VMEM((groups, layers * 5, lines, LANES), b16),
            pltpu.VMEM((groups, layers * 5, lines, LANES), b16),
            pltpu.VMEM((5, layers, share), f32),
            pltpu.VMEM((5, layers, channels), f32),
            pltpu.VMEM(train.shape, b16),
            pltpu.VMEM((train.shape[0], layers, share), f32),
            pltpu.SMEM(owner_map.shape, owner_map.dtype),
            dma((8,)), dma((groups,)),
            dma((3, groups)), dma((3, groups)),
            dma((count,)), dma((count,)), dma((groups,)), dma((groups,)), dma((groups,)), dma((groups,)),
            dma((count,)), dma((count,)),
        ],
        compiler_params=pltpu.CompilerParams(
            collective_id=0, has_side_effects=True, vmem_limit_bytes=63 << 20),
    )(owner_map, acts, cots, weights, bias, basis.reshape(25, tall, LANES), vals.reshape(5, tall, LANES), train)


def finish_kernel(pieces, a_hbm, v_hbm, i_hbm, out_hbm, s_hbm, held, v_ref, i_ref, s_ref, load, store, small):
    width = a_hbm.shape[0] // pieces
    slabs = [pl.ds(i * width, width) for i in range(pieces)]
    reads = [pltpu.make_async_copy(a_hbm.at[slab, :], held.at[slab, :], load.at[i]) for i, slab in enumerate(slabs)]
    writes = [pltpu.make_async_copy(held.at[slab, :], out_hbm.at[slab, :], store.at[i])
              for i, slab in enumerate(slabs)]
    loads = [pltpu.make_async_copy(v_hbm, v_ref, small.at[0]), pltpu.make_async_copy(i_hbm, i_ref, small.at[1])]
    for copy in reads + loads:
        copy.start()
    for copy, onward in zip(reads, writes):
        copy.wait()
        onward.start()
    for copy in loads:
        copy.wait()
    examples = v_ref.shape[0]
    picks = i_ref.shape[1]
    local = i_ref[...] - lax.axis_index("dp") * examples
    chosen = jnp.broadcast_to(local, (examples, picks)) == lax.broadcasted_iota(jnp.int32, (examples, picks), 0)
    s_ref[...] = jnp.sum(jnp.where(chosen, v_ref[:, :picks], 0.0), axis=0, keepdims=True)
    picked = pltpu.make_async_copy(s_ref, s_hbm, small.at[2])
    picked.start()
    for copy in writes:
        copy.wait()
    picked.wait()


def finish(moved, values, batch_index):
    picks = batch_index.shape[0]
    pieces = 8
    anywhere = pl.BlockSpec(memory_space=pltpu.HBM)
    return pl.pallas_call(
        functools.partial(finish_kernel, pieces),
        out_shape=(
            jax.ShapeDtypeStruct(moved.shape, moved.dtype),
            jax.ShapeDtypeStruct((1, picks), jnp.float32),
        ),
        in_specs=[anywhere] * 3,
        out_specs=(anywhere, anywhere),
        scratch_shapes=[
            pltpu.VMEM(moved.shape, moved.dtype),
            pltpu.VMEM(values.shape, values.dtype),
            pltpu.VMEM((1, picks), batch_index.dtype),
            pltpu.VMEM((1, picks), jnp.float32),
            pltpu.SemaphoreType.DMA((pieces,)),
            pltpu.SemaphoreType.DMA((pieces,)),
            pltpu.SemaphoreType.DMA((3,)),
        ],
        compiler_params=pltpu.CompilerParams(vmem_limit_bytes=63 << 20),
    )(moved, values, batch_index.reshape(1, picks))


def precondition_apart(query_acts, cotangent, conv_weight, conv_bias, owner_map, basis_store, lambda_store,
                       norm_scale):
    rows, channels = query_acts.shape
    layers = conv_weight.shape[0]
    here = lax.axis_index("dp")
    before = shifted(query_acts[rows - HALO_ROWS:], "dp", 1)
    after = shifted(jnp.concatenate([query_acts[:HALO_ROWS], cotangent[:HALO_ROWS]]), "dp", -1)
    halo_acts = jnp.concatenate([before, after[:HALO_ROWS]])
    halo_cots = jnp.concatenate([jnp.zeros_like(before), after[HALO_ROWS:]])
    own_rows = inverse_rows(basis_store[0], lambda_store[0])
    adjoint, partial = window(query_acts, cotangent, halo_acts, halo_cots, conv_weight, conv_bias)
    held = jnp.where((owner_map == here)[:, None, None], own_rows[None], 0.0)
    inverse = lax.psum(held, "dp")
    summed = (lax.psum(partial, "dp") * norm_scale).reshape(layers, 5, channels)
    order = {pair: i for i, pair in enumerate(PAIRS)}
    everyone = jnp.stack([
        sum(inverse[:, order[min(j, k), max(j, k)]] * summed[:, k] for k in range(5))
        for j in range(5)
    ], axis=1)
    return adjoint, everyone


def on_device(query_acts, cotangent, conv_weight, conv_bias, owner_map, basis_store, lambda_store,
              train_grads, batch_index):
    rows, channels = query_acts.shape
    layers = conv_weight.shape[0]
    count = lax.axis_size("dp")
    here = lax.axis_index("dp")
    norm_scale = 1.0 / math.sqrt(rows * count)
    lines = channels // (LANES * count)
    examples = train_grads.shape[0]
    final = 1.0 / math.sqrt(5 * layers * channels)
    if lines == 4 and count % 4 == 0 and channels == lines * LANES * count and (
            rows % HALO == 0 and batch_index.shape[0] <= LANES):
        moved, values = fused(query_acts, cotangent, conv_weight, conv_bias, owner_map, basis_store[0],
                                lambda_store[0], train_grads.transpose(0, 2, 1, 3), norm_scale, final)
        adjoint, scores = finish(moved, values, batch_index)
        return (adjoint, scores.reshape(-1))
    else:
        adjoint, everyone = precondition_apart(query_acts, cotangent, conv_weight, conv_bias, owner_map,
                                               basis_store, lambda_store, norm_scale)
        high = everyone.astype(jnp.bfloat16)
        low = (everyone - high.astype(jnp.float32)).astype(jnp.bfloat16)
        both = high.astype(jnp.float32) + low.astype(jnp.float32)
        values = jnp.sum(train_grads.astype(jnp.float32) * both[None], axis=(1, 2, 3)) * final
    local_index = batch_index - here * examples
    chosen = local_index[:, None] == jnp.arange(examples, dtype=jnp.int32)[None, :]
    scores = jnp.sum(jnp.where(chosen, values[None, :], 0.0), axis=1)
    return (adjoint, scores)


def solution(mesh):
    in_specs = (
        P(("groups", "dp"), None),
        P(("groups", "dp"), None),
        P(),
        P(),
        P(),
        P("dp", None, None),
        P("dp", None, None),
        P(("groups", "dp"), None, None, None),
        P(("groups", "dp")),
    )
    out_specs = (P(("groups", "dp"), None), P(("groups", "dp")))
    return jax.shard_map(
        on_device, mesh=mesh, in_specs=in_specs, out_specs=out_specs, check_vma=False
    )
```
